32 devices in a mesh: rows: 8 (over z, y), heads: 4 (over x, core).
Axes of the slice: x: 2, y: 2, z: 4, core: 2. Of those that a mesh axis runs over, the one named last changes fastest.
Arguments:
- token_ids: int32 [32, 256], P('rows'), may hold values from 0 to 50303
- lengths: int32 [32], P('rows'), may hold values from 40 to 256
- label_ids: int32 [32, 4], P('rows'), may hold values from 0 to 50303
- targets: float32 [32, 4], P('rows'), may hold values from -14 to -8
- step_count: int32 [1], replicated, may hold values from 2 to 20
- soap_owners: int32 [8], P('rows'), may hold values from 0 to 1
- soap_basis: float32 [4, 12, 64, 64], P(None, 'heads'), may hold values from -0.75 to 0.75
- table_anchor: bfloat16 [50304, 768], P(('heads', 'rows')), may hold values from -0.625 to 0.625
- table_delta: float32 [50304, 768], P(('heads', 'rows')), may hold values from -0.3125 to 0.3125
- table_first: float32 [50304, 768], P(('heads', 'rows')), may hold values from -0.00024414062 to 0.00024414062
- table_second: float32 [50304, 768], P(('heads', 'rows')), may hold values from 2.1874195e-11 to 8.749678e-11
- qkv_anchor: bfloat16 [3, 768, 768], P(None, 'rows', 'heads'), may hold values from -0.3125 to 0.3125
- qkv_delta: float32 [3, 768, 768], P(None, 'rows', 'heads'), may hold values from -0.21875 to 0.21875
- qkv_first: float32 [3, 768, 768], P(None, 'rows', 'heads'), may hold values from -0.00024414062 to 0.00024414062
- qkv_second: float32 [3, 768, 768], P(None, 'rows', 'heads'), may hold values from 2.1874195e-11 to 8.749678e-11
- out_anchor: bfloat16 [768, 768], P('heads', 'rows'), may hold values from -0.875 to 0.875
- out_delta: float32 [768, 768], P('heads', 'rows'), may hold values from -0.625 to 0.625
- out_first: float32 [768, 768], P('heads', 'rows'), may hold values from -0.00024414062 to 0.00024414062
- out_second: float32 [768, 768], P('heads', 'rows'), may hold values from 2.1874195e-11 to 8.749678e-11
- up_anchor: bfloat16 [768, 3072], P('rows', 'heads'), may hold values from -0.21875 to 0.21875
- up_delta: float32 [768, 3072], P('rows', 'heads'), may hold values from -0.15625 to 0.15625
- up_first: float32 [768, 3072], P('rows', 'heads'), may hold values from -0.00024414062 to 0.00024414062
- up_second: float32 [768, 3072], P('rows', 'heads'), may hold values from 2.1874195e-11 to 8.749678e-11
- down_anchor: bfloat16 [3072, 768], P('heads', 'rows'), may hold values from -0.21875 to 0.21875
- down_delta: float32 [3072, 768], P('heads', 'rows'), may hold values from -0.15625 to 0.15625
- down_first: float32 [3072, 768], P('heads', 'rows'), may hold values from -0.00024414062 to 0.00024414062
- down_second: float32 [3072, 768], P('heads', 'rows'), may hold values from 2.1874195e-11 to 8.749678e-11
- gain_anchor: float32 [3, 768], replicated, may hold values from 0.5 to 1.5
- gain_delta: float32 [3, 768], replicated, may hold values from -1.5 to 1.5
- gain_first: float32 [3, 768], replicated, may hold values from -0.0012207031 to 0.0012207031
- gain_second: float32 [3, 768], replicated, may hold values from 5.468549e-10 to 2.1874196e-09
- bias_anchor: float32 [3, 768], replicated, may hold values from -4 to 4
- bias_delta: float32 [3, 768], replicated, may hold values from -1.5 to 1.5
- bias_first: float32 [3, 768], replicated, may hold values from -0.0012207031 to 0.0012207031
- bias_second: float32 [3, 768], replicated, may hold values from 5.468549e-10 to 2.1874196e-09
Outputs:
- loss_value: float32 [], replicated
- new_table: float32 [50304, 768], P(('heads', 'rows'))
- new_table_first: float32 [50304, 768], P(('heads', 'rows'))
- new_table_second: float32 [50304, 768], P(('heads', 'rows'))
- new_qkv: float32 [3, 768, 768], P(None, 'rows', 'heads')
- new_qkv_first: float32 [3, 768, 768], P(None, 'rows', 'heads')
- new_qkv_second: float32 [3, 768, 768], P(None, 'rows', 'heads')
- new_out: float32 [768, 768], P('heads', 'rows')
- new_out_first: float32 [768, 768], P('heads', 'rows')
- new_out_second: float32 [768, 768], P('heads', 'rows')
- new_up: float32 [768, 3072], P('rows', 'heads')
- new_up_first: float32 [768, 3072], P('rows', 'heads')
- new_up_second: float32 [768, 3072], P('rows', 'heads')
- new_down: float32 [3072, 768], P('heads', 'rows')
- new_down_first: float32 [3072, 768], P('heads', 'rows')
- new_down_second: float32 [3072, 768], P('heads', 'rows')
- new_gain: float32 [3, 768], replicated
- new_gain_first: float32 [3, 768], replicated
- new_gain_second: float32 [3, 768], replicated
- new_bias: float32 [3, 768], replicated
- new_bias_first: float32 [3, 768], replicated
- new_bias_second: float32 [3, 768], replicated
The draws below stay inside these ranges and needn't reach their ends.
All inputs are finite; a program needn't handle non-finite values.
Results may differ from the reference program's by a relative error of at most 0.02.
Values may be sent and summed in bfloat16 or wider, within the bound.
No kernel may reach another device: no remote copies, remote signals or barrier semaphores. Data moves between devices by JAX's collectives and lax.ppermute only.
A program may use at most 256 MiB of HBM per device.

```python
import math
import jax
import jax.numpy as jnp
import numpy as np
from jax import lax

D = 768
NHEAD = 12
HDIM = 64
FF = 3072
VOCAB = 50304
SEQ = 256
NLW = 4
CGIT = 8
P_DEV = 1
PROMPTS = 32
BLOCKS = 8
NPARS = 45715968
N_ROWS = 8
N_HEADS = 4


def set_ends(drawn, own_key, low, largest):
    index_at = [jax.random.randint(jax.random.fold_in(own_key, axis), (), 0, length) for axis, length in enumerate(drawn.shape)]
    longest = drawn.shape.index(max(drawn.shape))
    neighbour = index_at[:longest] + [(index_at[longest] + 1) % drawn.shape[longest]] + index_at[longest + 1:]
    return drawn.at[tuple(index_at)].set(low).at[tuple(neighbour)].set(largest)


def shard_levels(rng, shape, shards, low, high):
    level, own = 1.0, jax.random.fold_in(rng, 6)
    for position, blocks in shards:
        heights = jnp.exp(jax.random.uniform(jax.random.fold_in(own, position), (blocks,), jnp.float32, low / len(shards), high / len(shards)))
        level = level * jnp.repeat(heights, shape[position] // blocks).reshape([-1 if axis == position else 1 for axis in range(len(shape))])
    return level


def rank_bounds(number_of, slope):
    loads = [(1 << 20) // math.isqrt(rank ** slope) + 1 for rank in range(1, number_of + 1)]
    deviation = 1 + sum(loads) // (1 << 30)
    return np.cumsum(np.array([max(1, weight // deviation) for weight in loads]))


def skewed_ids(key, dims, count, skew):
    listing = rank_bounds(count, skew)
    ticket = jax.random.randint(jax.random.fold_in(key, 1), dims, 0, int(listing[count - 1]))
    rank = jnp.searchsorted(jnp.asarray(listing, jnp.int32), ticket, side="right")
    return jax.random.permutation(jax.random.fold_in(key, 2), count)[rank].astype(jnp.int32)


def noise(key, extent, deviation, bound, cuts=(), kind=jnp.bfloat16):
    factor_of = shard_levels(key, extent, cuts, -0.22, 0.18) if cuts else 1.0
    result = jax.random.normal(key, extent, jnp.float32) * deviation * factor_of
    return jnp.minimum(jnp.maximum(result, -bound), bound).astype(kind)


def setup_inputs(seed: int = 0) -> dict:
    seeds = jax.random.split(jax.random.key(seed), 36)
    token_ids = set_ends(skewed_ids(seeds[0], (PROMPTS, SEQ), VOCAB, 2), jax.random.fold_in(seeds[0], 3), 0, VOCAB - 1).astype(jnp.int32)
    lengths = set_ends(jax.random.randint(seeds[1], (PROMPTS,), SEQ * 5 // 32, SEQ + 1), jax.random.fold_in(seeds[1], 1), SEQ * 5 // 32, SEQ).astype(jnp.int32)
    label_ids = set_ends(jax.random.randint(seeds[2], (PROMPTS, NLW), 0, VOCAB), jax.random.fold_in(seeds[2], 1), 0, VOCAB - 1).astype(jnp.int32)
    targets = jnp.clip(-14.0 + 6.0 * jax.random.uniform(seeds[3], (PROMPTS, NLW), jnp.float32) ** shard_levels(seeds[3], (PROMPTS, NLW), ((0, 8),), -0.2, 0.2), -14.0, -8.0)
    step_count = jax.random.randint(seeds[4], (1,), 2, 21).astype(jnp.int32)
    soap_owners = set_ends(jax.random.randint(seeds[5], (BLOCKS,), 0, 2), jax.random.fold_in(seeds[5], 1), 0, 1).astype(jnp.int32)
    soap_basis = noise(seeds[6], (4, NHEAD, HDIM, HDIM), HDIM ** -0.5, 0.75, ((1, 4),), jnp.float32)
    table_anchor = noise(seeds[7], (VOCAB, D), (D // 10) ** -0.5, 0.625, ((0, 32),))
    table_delta = noise(seeds[8], (VOCAB, D), (0.6 / D ** 0.5), 0.3125, ((0, 32),), jnp.float32)
    table_first = noise(seeds[9], (VOCAB, D), (0.11 / NPARS ** 0.5), 0.00024414062, ((0, 32),), jnp.float32)
    table_second = jnp.clip(2.1874195163529286e-11 + 6.562258549058786e-11 * jax.random.uniform(seeds[10], (VOCAB, D), jnp.float32) ** shard_levels(seeds[10], (VOCAB, D), ((0, 32),), -0.2, 0.2), 2.1874195163529286e-11, 8.749678065411715e-11)
    qkv_anchor = noise(seeds[11], (3, D, D), (D // 2) ** -0.5, 0.3125, ((1, 8), (2, 4)))
    qkv_delta = noise(seeds[12], (3, D, D), (0.4 / D ** 0.5), 0.21875, ((1, 8), (2, 4)), jnp.float32)
    qkv_first = noise(seeds[13], (3, D, D), (0.11 / NPARS ** 0.5), 0.00024414062, ((1, 8), (2, 4)), jnp.float32)
    qkv_second = jnp.clip(2.1874195163529286e-11 + 6.562258549058786e-11 * jax.random.uniform(seeds[14], (3, D, D), jnp.float32) ** shard_levels(seeds[14], (3, D, D), ((1, 8), (2, 4)), -0.2, 0.2), 2.1874195163529286e-11, 8.749678065411715e-11)
    out_anchor = noise(seeds[15], (D, D), (D // 16) ** -0.5, 0.875, ((0, 4), (1, 8)))
    out_delta = noise(seeds[16], (D, D), (1.2 / D ** 0.5), 0.625, ((0, 4), (1, 8)), jnp.float32)
    out_first = noise(seeds[17], (D, D), (0.11 / NPARS ** 0.5), 0.00024414062, ((0, 4), (1, 8)), jnp.float32)
    out_second = jnp.clip(2.1874195163529286e-11 + 6.562258549058786e-11 * jax.random.uniform(seeds[18], (D, D), jnp.float32) ** shard_levels(seeds[18], (D, D), ((0, 4), (1, 8)), -0.2, 0.2), 2.1874195163529286e-11, 8.749678065411715e-11)
    up_anchor = noise(seeds[19], (D, FF), D ** -0.5, 0.21875, ((0, 8), (1, 4)))
    up_delta = noise(seeds[20], (D, FF), (0.3 / D ** 0.5), 0.15625, ((0, 8), (1, 4)), jnp.float32)
    up_first = noise(seeds[21], (D, FF), (0.11 / NPARS ** 0.5), 0.00024414062, ((0, 8), (1, 4)), jnp.float32)
    up_second = jnp.clip(2.1874195163529286e-11 + 6.562258549058786e-11 * jax.random.uniform(seeds[22], (D, FF), jnp.float32) ** shard_levels(seeds[22], (D, FF), ((0, 8), (1, 4)), -0.2, 0.2), 2.1874195163529286e-11, 8.749678065411715e-11)
    down_anchor = noise(seeds[23], (FF, D), (FF // 4) ** -0.5, 0.21875, ((0, 4), (1, 8)))
    down_delta = noise(seeds[24], (FF, D), (0.6 / FF ** 0.5), 0.15625, ((0, 4), (1, 8)), jnp.float32)
    down_first = noise(seeds[25], (FF, D), (0.11 / NPARS ** 0.5), 0.00024414062, ((0, 4), (1, 8)), jnp.float32)
    down_second = jnp.clip(2.1874195163529286e-11 + 6.562258549058786e-11 * jax.random.uniform(seeds[26], (FF, D), jnp.float32) ** shard_levels(seeds[26], (FF, D), ((0, 4), (1, 8)), -0.2, 0.2), 2.1874195163529286e-11, 8.749678065411715e-11)
    gain_anchor = jnp.clip(1.0 + 0.1 * jax.random.normal(seeds[27], (3, D), jnp.float32), 0.5, 1.5)
    gain_delta = noise(seeds[28], (3, D), 0.1, 1.5, (), jnp.float32)
    gain_first = noise(seeds[29], (3, D), (0.55 / NPARS ** 0.5), 0.0012207031, (), jnp.float32)
    gain_second = jnp.clip(jax.random.uniform(seeds[30], (3, D), jnp.float32, 5.468548947007434e-10, 2.1874195788029738e-09), 5.468548947007434e-10, 2.1874195788029738e-09)
    bias_anchor = noise(seeds[31], (3, D), 0.3, 4.0, (), jnp.float32)
    bias_delta = noise(seeds[32], (3, D), 0.1, 1.5, (), jnp.float32)
    bias_first = noise(seeds[33], (3, D), (0.55 / NPARS ** 0.5), 0.0012207031, (), jnp.float32)
    bias_second = jnp.clip(jax.random.uniform(seeds[34], (3, D), jnp.float32, 5.468548947007434e-10, 2.1874195788029738e-09), 5.468548947007434e-10, 2.1874195788029738e-09)
    return {"token_ids": token_ids, "lengths": lengths, "label_ids": label_ids, "targets": targets, "step_count": step_count, "soap_owners": soap_owners, "soap_basis": soap_basis, "table_anchor": table_anchor, "table_delta": table_delta, "table_first": table_first, "table_second": table_second, "qkv_anchor": qkv_anchor, "qkv_delta": qkv_delta, "qkv_first": qkv_first, "qkv_second": qkv_second, "out_anchor": out_anchor, "out_delta": out_delta, "out_first": out_first, "out_second": out_second, "up_anchor": up_anchor, "up_delta": up_delta, "up_first": up_first, "up_second": up_second, "down_anchor": down_anchor, "down_delta": down_delta, "down_first": down_first, "down_second": down_second, "gain_anchor": gain_anchor, "gain_delta": gain_delta, "gain_first": gain_first, "gain_second": gain_second, "bias_anchor": bias_anchor, "bias_delta": bias_delta, "bias_first": bias_first, "bias_second": bias_second}


@jax.custom_vjp
def low(v):
    return lax.optimization_barrier(v.astype(jnp.bfloat16)).astype(jnp.float32)

@jax.custom_vjp
def low_back(v):
    return v

def low_keep(v):
    return (low(v), None)

def low_pass(kept, grad):
    return (grad,)

def back_keep(v):
    return (v, None)

def back_low(kept, grad):
    return (low(grad),)
low.defvjp(low_keep, low_pass)
low_back.defvjp(back_keep, back_low)
EPS_NORM = 1e-05
BETA_ONE = 0.9
BETA_TWO = 0.999
ADAM_EPS = 1e-08
LEARN_RATE = 0.03
DECAY_RATE = 0.01
CLIP_NORM = 1.0
CG_SHIFT = 0.002
MASKED = -1e+30
HALF_ROOT = 0.7071067811865476
INV_ROOT_TAU = 0.3989422804014327
HIGH = lax.Precision.HIGHEST

def product(left, right):
    return jnp.dot(left, right, precision=HIGH, preferred_element_type=jnp.float32)

def round_both(values):
    return low_back(low(values))

def gelu_slope(values):
    return 0.5 * (1.0 + lax.erf(values * HALF_ROOT)) + values * jnp.exp(-0.5 * values * values) * INV_ROOT_TAU

def norm_pair(values, dots, gain, bias, gain_dot, bias_dot):
    center = values - lax.optimization_barrier(jnp.mean(values, axis=-1, keepdims=True))
    inverse = lax.rsqrt(lax.optimization_barrier(jnp.mean(center * center, axis=-1, keepdims=True)) + EPS_NORM)
    normed = center * inverse
    normed_dot = inverse * (dots - lax.optimization_barrier(jnp.mean(dots, axis=-1, keepdims=True)) - normed * lax.optimization_barrier(jnp.mean(normed * dots, axis=-1, keepdims=True)))
    return (normed * gain + bias, normed_dot * gain + normed * gain_dot + bias_dot)

def group_outputs(steps_in, anchors, token_ids, lengths, label_ids):
    table_step, qkv_step, out_step, up_step, down_step, gain_dot, bias_dot = steps_in
    table, qkv_w, out_w, up_w, down_w, gain, bias = anchors
    prompts = token_ids.shape[0]
    flat_ids = token_ids.reshape(-1)
    embedded = table[flat_ids]
    embedded_dot = low_back(table_step[flat_ids])
    start_x, start_dot = norm_pair(embedded, embedded_dot, gain[0], bias[0], gain_dot[0], bias_dot[0])
    attn_in = low(start_x)
    attn_dot_in = low(start_dot)
    projected = [low(product(attn_in, qkv_w[index])).reshape(prompts, SEQ, NHEAD, HDIM) for index in range(3)]
    projected_dot = [round_both(product(attn_dot_in, qkv_w[index]) + product(attn_in, qkv_step[index])).reshape(prompts, SEQ, NHEAD, HDIM) for index in range(3)]
    scale = HDIM ** (-0.5)
    scores = jnp.einsum('gqhd,gkhd->ghqk', projected[0], projected[1], precision=HIGH) * scale
    live_keys = jnp.arange(SEQ)[None, :] < lengths[:, None]
    scores = jnp.where(live_keys[:, None, None, :], scores, MASKED)
    probs = jax.nn.softmax(scores, axis=-1)
    probs_low = low(probs)
    score_dot = jnp.einsum('gqhd,gkhd->ghqk', projected_dot[0], projected[1], precision=HIGH)
    score_dot = low_back((score_dot + jnp.einsum('gqhd,gkhd->ghqk', projected[0], projected_dot[1], precision=HIGH)) * scale)
    prob_dot = low(probs * (score_dot - lax.optimization_barrier(jnp.sum(probs * score_dot, axis=-1, keepdims=True))))
    attended = low(jnp.einsum('ghqk,gkhd->gqhd', probs_low, projected[2], precision=HIGH)).reshape(prompts * SEQ, D)
    attended_dot = jnp.einsum('ghqk,gkhd->gqhd', prob_dot, projected[2], precision=HIGH)
    attended_dot = round_both(attended_dot + jnp.einsum('ghqk,gkhd->gqhd', probs_low, projected_dot[2], precision=HIGH)).reshape(prompts * SEQ, D)
    attn_out = product(attended, out_w)
    attn_dot = low_back(product(attended_dot, out_w) + product(attended, out_step))
    hidden, hidden_dot = norm_pair(start_x + attn_out, start_dot + attn_dot, gain[1], bias[1], gain_dot[1], bias_dot[1])
    hidden_low = low(hidden)
    pre_gelu = product(hidden_low, up_w)
    pre_dot = low_back(product(low(hidden_dot), up_w) + product(hidden_low, up_step))
    activated = low(jax.nn.gelu(pre_gelu, approximate=False))
    act_dot = low(gelu_slope(pre_gelu) * pre_dot)
    ffn_out = product(activated, down_w)
    ffn_dot = low_back(product(act_dot, down_w) + product(activated, down_step))
    final_out, final_dot = norm_pair(hidden + ffn_out, hidden_dot + ffn_dot, gain[2], bias[2], gain_dot[2], bias_dot[2])
    final_out = final_out.reshape(prompts, SEQ, D)
    final_dot = final_dot.reshape(prompts, SEQ, D)
    length_float = lengths.astype(jnp.float32)[:, None]
    feat = low(lax.optimization_barrier(jnp.sum(jnp.where(live_keys[:, :, None], final_out, 0.0), axis=1)) / length_float)
    feat_dot = low(lax.optimization_barrier(jnp.sum(jnp.where(live_keys[:, :, None], final_dot, 0.0), axis=1)) / length_float)
    logits = product(feat, table.T)
    logit_dot = low_back(product(feat_dot, table.T) + product(feat, table_step.T))
    log_norm = jax.nn.logsumexp(logits, axis=-1, keepdims=True)
    softmax_all = jnp.exp(logits - log_norm)
    picked = jnp.take_along_axis(logits, label_ids, axis=1) - log_norm
    picked_dot = jnp.take_along_axis(logit_dot, label_ids, axis=1) - lax.optimization_barrier(jnp.sum(softmax_all * logit_dot, axis=-1, keepdims=True))
    return (picked + picked_dot, feat)

def all_outputs(steps_in, anchors, token_ids, lengths, label_ids):
    groups = token_ids.shape[0] // (P_DEV * N_HEADS)
    pieces = (token_ids.reshape(groups, -1, SEQ), lengths.reshape(groups, -1), label_ids.reshape(groups, -1, NLW))

    def one_group(piece):
        return group_outputs(steps_in, anchors, piece[0], piece[1], piece[2])
    linear, feat = lax.map(jax.checkpoint(one_group), pieces)
    return (linear.reshape(-1, NLW), feat.reshape(-1, D))

def kernel_solve(features, right_side):
    centered = features - lax.optimization_barrier(jnp.mean(features, axis=0, keepdims=True))

    def apply(vector):
        return product(centered, product(centered.T, vector)) / D + CG_SHIFT * vector
    solution = jnp.zeros_like(right_side)
    residual = right_side
    direction = right_side
    norm_now = lax.optimization_barrier(jnp.sum(residual * residual, axis=0))
    for step in range(CGIT):
        image = apply(direction)
        alpha = norm_now / lax.optimization_barrier(jnp.sum(direction * image, axis=0))
        solution = solution + alpha * direction
        residual = residual - alpha * image
        norm_next = lax.optimization_barrier(jnp.sum(residual * residual, axis=0))
        direction = residual + norm_next / norm_now * direction
        norm_now = norm_next
    return solution

def adam_moments(gradient, moment_one, moment_two, bias_one, bias_two):
    new_one = BETA_ONE * moment_one + (1.0 - BETA_ONE) * gradient
    new_two = BETA_TWO * moment_two + (1.0 - BETA_TWO) * gradient * gradient
    return (new_one / bias_one / (jnp.sqrt(new_two / bias_two) + ADAM_EPS), new_one, new_two)

def adam_update(master, gradient, moment_one, moment_two, clip_scale, bias_one, bias_two):
    direction, new_one, new_two = adam_moments(clip_scale * gradient, moment_one, moment_two, bias_one, bias_two)
    return (master - LEARN_RATE * (direction + DECAY_RATE * master), new_one, new_two)

def soap_columns(master, gradient, moment_one, moment_two, basis, clip_scale, bias_one, bias_two):
    height = gradient.shape[0]
    groups = basis.shape[0]
    split = (clip_scale * gradient).reshape(height, groups, HDIM)
    turned = jnp.einsum('iha,hab->ihb', split, basis, precision=HIGH).reshape(height, groups * HDIM)
    direction, new_one, new_two = adam_moments(turned, moment_one, moment_two, bias_one, bias_two)
    back = jnp.einsum('ihb,hab->iha', direction.reshape(height, groups, HDIM), basis, precision=HIGH).reshape(height, groups * HDIM)
    return (master - LEARN_RATE * (back + DECAY_RATE * master), new_one, new_two)

def reference(token_ids, lengths, label_ids, targets, step_count, soap_owners, soap_basis, table_anchor, table_delta, table_first, table_second, qkv_anchor, qkv_delta, qkv_first, qkv_second, out_anchor, out_delta, out_first, out_second, up_anchor, up_delta, up_first, up_second, down_anchor, down_delta, down_first, down_second, gain_anchor, gain_delta, gain_first, gain_second, bias_anchor, bias_delta, bias_first, bias_second):
    anchors = tuple((array.astype(jnp.float32) for array in (table_anchor, qkv_anchor, out_anchor, up_anchor, down_anchor))) + (gain_anchor, bias_anchor)
    deltas = (table_delta, qkv_delta, out_delta, up_delta, down_delta, gain_delta, bias_delta)

    def outputs_of(*values):
        lowered = tuple((low(value) for value in values[:5])) + tuple(values[5:])
        return all_outputs(lowered, anchors, token_ids, lengths, label_ids)
    (linear, features), pullback = jax.vjp(outputs_of, *deltas)
    differ = linear - targets
    loss_value = jnp.sum(differ * differ) / NLW
    solution = kernel_solve(features, differ)
    grads = pullback((2.0 * solution / NLW, jnp.zeros_like(features)))
    squares = sum((jnp.sum(gradient * gradient) for gradient in grads))
    clip_scale = jnp.minimum(1.0, CLIP_NORM / jnp.sqrt(squares))
    count = step_count[0].astype(jnp.float32)
    bias_one = 1.0 - jnp.power(BETA_ONE, count)
    bias_two = 1.0 - jnp.power(BETA_TWO, count)
    firsts = (table_first, qkv_first, out_first, up_first, down_first, gain_first, bias_first)
    seconds = (table_second, qkv_second, out_second, up_second, down_second, gain_second, bias_second)
    results = [adam_update(deltas[index], grads[index], firsts[index], seconds[index], clip_scale, bias_one, bias_two) for index in range(7)]
    flags = jnp.repeat(soap_owners, D // N_ROWS) == 1
    qkv_parts = [soap_columns(qkv_delta[index], grads[1][index], qkv_first[index], qkv_second[index], soap_basis[index], clip_scale, bias_one, bias_two) for index in range(3)]
    qkv_soap = tuple((jnp.stack([part[member] for part in qkv_parts]) for member in range(3)))
    results[1] = tuple((jnp.where(flags[None, :, None], qkv_soap[member], results[1][member]) for member in range(3)))
    out_soap = soap_columns(out_delta.T, grads[2].T, out_first.T, out_second.T, soap_basis[3], clip_scale, bias_one, bias_two)
    results[2] = tuple((jnp.where(flags[None, :], out_soap[member].T, results[2][member]) for member in range(3)))
    flat = [loss_value]
    for triple in results:
        flat.extend(triple)
    return (flat[0], flat[1], flat[2], flat[3], flat[4], flat[5], flat[6], flat[7], flat[8], flat[9], flat[10], flat[11], flat[12], flat[13], flat[14], flat[15], flat[16], flat[17], flat[18], flat[19], flat[20], flat[21])
```

```python
import jax
import jax.numpy as jnp
from jax import lax
from jax.experimental import pallas as pl
from jax.sharding import PartitionSpec as P

D = 768
HDIM = 64
SEQ = 256
NLW = 4
CGIT = 8
STATS = 16

EPS_NORM = 1e-05
BETA_ONE = 0.9
BETA_TWO = 0.999
ADAM_EPS = 1e-08
LEARN_RATE = 0.03
DECAY_RATE = 0.01
CLIP_NORM = 1.0
CG_SHIFT = 0.002
MASKED = -1e30
HALF_ROOT = 0.7071067811865476
INV_ROOT_TAU = 0.3989422804014327
HIGH = lax.Precision.HIGHEST
ALL = ("heads", "rows")
LOW = jnp.bfloat16


def einsum(form, left, right):
    return jnp.einsum(form, left, right, preferred_element_type=jnp.float32)


def gelu_slope(values):
    return (
        0.5 * (1.0 + lax.erf(values * HALF_ROOT))
        + values * jnp.exp(-0.5 * values * values) * INV_ROOT_TAU
    )


def norm_pair(values, dots, gain, bias, gain_dot, bias_dot):
    center = values - jnp.mean(values, axis=-1, keepdims=True)
    inverse = lax.rsqrt(jnp.mean(center * center, axis=-1, keepdims=True) + EPS_NORM)
    normed = center * inverse
    normed_dot = inverse * (
        dots
        - jnp.mean(dots, axis=-1, keepdims=True)
        - normed * jnp.mean(normed * dots, axis=-1, keepdims=True)
    )
    return (normed * gain + bias, normed_dot * gain + normed * gain_dot + bias_dot, normed, inverse)


def norm_backward(grad_out, normed, inverse, gain):
    scaled = grad_out * gain
    grad_in = inverse * (
        scaled
        - jnp.mean(scaled, axis=-1, keepdims=True)
        - normed * jnp.mean(scaled * normed, axis=-1, keepdims=True)
    )
    return (grad_in, jnp.sum(grad_out * normed, axis=0), jnp.sum(grad_out, axis=0))


def partners(axis):
    size = lax.axis_size(axis)
    bit = 1
    while bit < size:
        yield bit, [(index, index ^ bit) for index in range(size)]
        bit *= 2


def spread(block):
    for axis in reversed(ALL):
        here = lax.axis_index(axis)
        for bit, pairs in partners(axis):
            other = lax.ppermute(block, axis, pairs)
            block = jnp.where(
                (here & bit) > 0,
                jnp.concatenate([other, block]),
                jnp.concatenate([block, other]),
            )
    return block


def total(values, combine=jnp.add):
    for axis in reversed(ALL):
        for _, pairs in partners(axis):
            values = jax.tree.map(
                lambda part: combine(part, lax.ppermute(part, axis, pairs)), values
            )
    return values


def solve_kernel(stats_ref, feat_ref, targets_ref, coef_ref, norm_ref, loss_ref):
    count = feat_ref.shape[0]

    def stat(index):
        return stats_ref[:, index * count : (index + 1) * count]

    peaks = stat(0)
    peak = jnp.max(peaks, axis=0, keepdims=True)
    scale = jnp.exp(peaks - peak)
    mass = jnp.sum(stat(1) * scale, axis=0, keepdims=True)
    weighted = jnp.sum(stat(2) * scale, axis=0, keepdims=True)
    log_norm = peak + jnp.log(mass)
    shift = log_norm + weighted / mass
    picked = [
        jnp.sum(stat(3 + word) + stat(3 + NLW + word), axis=0, keepdims=True)
        for word in range(NLW)
    ]
    differ = jnp.concatenate(picked, axis=0) - shift - targets_ref[...]
    feat = feat_ref[...].astype(jnp.float32)
    center = feat - jnp.mean(feat, axis=0, keepdims=True)
    kernel = (
        lax.dot_general(
            center,
            center,
            (((1,), (1,)), ((), ())),
            precision=HIGH,
            preferred_element_type=jnp.float32,
        )
        / D
    )
    answer = jnp.zeros_like(differ)
    residual = differ
    direction = differ
    norm_now = jnp.sum(residual * residual, axis=1, keepdims=True)
    for step in range(CGIT):
        image = (
            jnp.dot(direction, kernel, precision=HIGH, preferred_element_type=jnp.float32)
            + CG_SHIFT * direction
        )
        alpha = norm_now / jnp.sum(direction * image, axis=1, keepdims=True)
        answer = answer + alpha * direction
        residual = residual - alpha * image
        if step + 1 < CGIT:
            norm_next = jnp.sum(residual * residual, axis=1, keepdims=True)
            direction = residual + norm_next / norm_now * direction
            norm_now = norm_next
    coef_ref[...] = 2.0 * answer / NLW
    norm_ref[...] = log_norm
    squares = jnp.sum(differ * differ, axis=1, keepdims=True)
    loss_ref[...] = jnp.sum(squares, axis=0, keepdims=True) / NLW


def solve(stats, feat, targets):
    count = feat.shape[0]
    return pl.pallas_call(
        solve_kernel,
        out_shape=(
            jax.ShapeDtypeStruct((NLW, count), jnp.float32),
            jax.ShapeDtypeStruct((1, count), jnp.float32),
            jax.ShapeDtypeStruct((1, 1), jnp.float32),
        ),
    )(stats, feat, targets)


def adam_moments(gradient, moment_one, moment_two, bias_one, bias_two):
    new_one = BETA_ONE * moment_one + (1.0 - BETA_ONE) * gradient
    new_two = BETA_TWO * moment_two + (1.0 - BETA_TWO) * gradient * gradient
    return (new_one / bias_one / (jnp.sqrt(new_two / bias_two) + ADAM_EPS), new_one, new_two)


def adam_update(master, gradient, moment_one, moment_two, clip_scale, bias_one, bias_two):
    direction, new_one, new_two = adam_moments(
        clip_scale * gradient, moment_one, moment_two, bias_one, bias_two
    )
    return (master - LEARN_RATE * (direction + DECAY_RATE * master), new_one, new_two)


def turned_update(owner, master, gradient, first, second, basis, clip_scale, bias_one, bias_two):
    count, height, width = gradient.shape

    def grouped(array):
        return array.reshape(count, height, width // HDIM, HDIM)

    plain = clip_scale * gradient
    turned = jnp.einsum("ciha,chab->cihb", grouped(plain), basis, precision=HIGH)
    used = jnp.where(owner, turned.reshape(gradient.shape), plain)
    direction, new_one, new_two = adam_moments(used, first, second, bias_one, bias_two)
    back = jnp.einsum("cihb,chab->ciha", grouped(direction), basis, precision=HIGH)
    direction = jnp.where(owner, back.reshape(gradient.shape), direction)
    return (master - LEARN_RATE * (direction + DECAY_RATE * master), new_one, new_two)


def per_device(
    token_ids,
    lengths,
    label_ids,
    targets,
    step_count,
    soap_owners,
    soap_basis,
    table_anchor,
    table_delta,
    table_first,
    table_second,
    qkv_anchor,
    qkv_delta,
    qkv_first,
    qkv_second,
    out_anchor,
    out_delta,
    out_first,
    out_second,
    up_anchor,
    up_delta,
    up_first,
    up_second,
    down_anchor,
    down_delta,
    down_first,
    down_second,
    gain_anchor,
    gain_delta,
    gain_first,
    gain_second,
    bias_anchor,
    bias_delta,
    bias_first,
    bias_second,
):
    n_heads = lax.axis_size("heads")
    n_rows = lax.axis_size("rows")
    count = n_heads * n_rows
    head_index = lax.axis_index("heads")
    me = head_index * n_rows + lax.axis_index("rows")
    vocab = table_anchor.shape[0]
    group_wide = qkv_anchor.shape[2]
    local_heads = group_wide // HDIM

    def side_by_side(qkv, out):
        return jnp.concatenate([qkv[0], qkv[1], qkv[2], out.T], axis=1)

    def gathered(anchor, delta):
        block = jnp.concatenate([anchor, delta.astype(LOW)], axis=1)
        full = lax.all_gather(block, ALL, axis=0, tiled=True)
        return full.reshape(n_heads, D, block.shape[1])

    attn_all = gathered(side_by_side(qkv_anchor, out_anchor), side_by_side(qkv_delta, out_delta))
    up_all = gathered(up_anchor, up_delta)
    down_all = gathered(down_anchor.T, down_delta.T)

    room = 8 * -(-(2 * SEQ // count + 8) // 8)
    slots = count * room
    ids = lax.dynamic_index_in_dim(token_ids, head_index, 0, keepdims=False)
    owner = ids // vocab
    local = ids - owner * vocab
    place = lax.iota(jnp.int32, SEQ)
    same = ids[:, None] == ids[None, :]
    earliest = jnp.min(jnp.where(same, place[None, :], SEQ), axis=1)
    leads = earliest == place
    rank = jnp.sum(
        (leads[None, :] & (owner[:, None] == owner[None, :]) & (place[None, :] < earliest[:, None])),
        axis=1,
        dtype=jnp.int32,
    )
    longest = jnp.max(rank) + 1
    rounds = -(-total(longest.reshape(1, 1), jnp.maximum)[0, 0] // room)
    both = jnp.concatenate([table_anchor, table_delta.astype(LOW)], axis=1)

    def slot_of(turn):
        within = rank - turn * room
        return jnp.where((within >= 0) & (within < room), owner * room + within, -1)

    def asked(turn):
        taken = jnp.where(leads, slot_of(turn), -1)
        hit = lax.iota(jnp.int32, slots)[:, None] == taken[None, :]
        wanted = jnp.sum(jnp.where(hit, local[None, :] + 1, 0), axis=1) - 1
        wanted = lax.all_to_all(wanted.reshape(count, room), ALL, 0, 0, tiled=True)
        return wanted.reshape(slots)

    def chosen(wanted):
        return (wanted[:, None] == lax.broadcasted_iota(jnp.int32, (slots, vocab), 1)).astype(LOW)

    def token_slots(turn):
        return (
            slot_of(turn)[:, None] == lax.broadcasted_iota(jnp.int32, (SEQ, slots), 1)
        ).astype(LOW)

    def fetch(turn, wanted):
        rows = einsum("sv,vd->sd", chosen(wanted), both).astype(LOW)
        rows = lax.all_to_all(rows.reshape(count, room, 2 * D), ALL, 0, 0, tiled=True)
        return einsum("ts,sd->td", token_slots(turn), rows.reshape(slots, 2 * D))

    def give(turn, wanted, grads):
        sums = einsum("ts,td->sd", token_slots(turn), grads).astype(LOW)
        sums = lax.all_to_all(sums.reshape(count, room, D), ALL, 0, 0, tiled=True)
        return einsum("sv,sd->vd", chosen(wanted), sums.reshape(slots, D))

    def more(start, step):
        def rest(value):
            return lax.fori_loop(1, rounds, lambda turn, so_far: so_far + step(turn), value)

        return lax.cond(rounds > 1, rest, lambda value: value, start)

    wanted_first = asked(0)
    embedded_both = more(fetch(0, wanted_first), lambda turn: fetch(turn, asked(turn)))
    start_x, start_dot, normed_zero, inverse_zero = norm_pair(
        embedded_both[:, :D],
        embedded_both[:, D:],
        gain_anchor[0],
        bias_anchor[0],
        gain_delta[0],
        bias_delta[0],
    )

    own_length = lax.dynamic_index_in_dim(lengths, head_index, 0, keepdims=False)
    live = lax.iota(jnp.int32, SEQ) < own_length
    length_float = own_length.astype(jnp.float32)

    notes = jnp.concatenate([label_ids.astype(jnp.float32), targets], axis=1)
    notes = jnp.swapaxes(lax.all_gather(notes, "rows"), 0, 1).reshape(count, 2 * NLW)
    labels = notes[:, :NLW].astype(jnp.int32) - me * vocab
    targets_all = notes[:, NLW:].T

    attn_in = start_x.astype(LOW)
    attn_dot_in = start_dot.astype(LOW)
    three = 3 * group_wide
    wide = attn_all.shape[2] // 2
    through = einsum("td,hde->the", attn_in, attn_all)
    projected = through[:, :, :three].astype(LOW)
    projected_dot = (
        through[:, :, wide : wide + three]
        + einsum("td,hde->the", attn_dot_in, attn_all[:, :, :three])
    ).astype(LOW)

    def split_heads(array):
        array = array.reshape(SEQ, n_heads, 3, local_heads, HDIM)
        return [array[:, :, index].reshape(SEQ, n_heads * local_heads, HDIM) for index in range(3)]

    query, key, value = split_heads(projected)
    query_dot, key_dot, value_dot = split_heads(projected_dot)
    scores = einsum("qhd,khd->hqk", query, key) * HDIM ** (-0.5)
    scores = jnp.where(live[None, None, :], scores, MASKED)
    exponent = jnp.exp(scores - jnp.max(scores, axis=-1, keepdims=True))
    probs = exponent / jnp.sum(exponent, axis=-1, keepdims=True)
    probs_low = probs.astype(LOW)
    score_dot = (
        einsum("qhd,khd->hqk", query_dot, key) + einsum("qhd,khd->hqk", query, key_dot)
    ) * HDIM ** (-0.5)
    prob_dot = (probs * (score_dot - jnp.sum(probs * score_dot, axis=-1, keepdims=True))).astype(LOW)
    attended = einsum("hqk,khd->qhd", probs_low, value).astype(LOW)
    attended_dot = (
        einsum("hqk,khd->qhd", prob_dot, value) + einsum("hqk,khd->qhd", probs_low, value_dot)
    ).astype(LOW)
    attended = attended.reshape(SEQ, n_heads, group_wide)
    attended_dot = attended_dot.reshape(SEQ, n_heads, group_wide)
    out_full = attn_all[:, :, three:wide]
    out_step = attn_all[:, :, wide + three :]
    attn_out = einsum("the,hde->td", attended, out_full)
    attn_dot = einsum("the,hde->td", attended_dot, out_full) + einsum(
        "the,hde->td", attended, out_step
    )
    hidden, hidden_dot, normed_one, inverse_one = norm_pair(
        start_x + attn_out,
        start_dot + attn_dot,
        gain_anchor[1],
        bias_anchor[1],
        gain_delta[1],
        bias_delta[1],
    )
    ffn_input = hidden.astype(LOW)
    half = up_all.shape[2] // 2
    up_full = up_all[:, :, :half]
    down_full = down_all[:, :, :half]
    through = einsum("td,hde->the", ffn_input, up_all)
    pre_gelu = through[:, :, :half]
    pre_dot = through[:, :, half:] + einsum("td,hde->the", hidden_dot.astype(LOW), up_full)
    activated = jax.nn.gelu(pre_gelu, approximate=False).astype(LOW)
    slope = gelu_slope(pre_gelu)
    act_dot = (slope * pre_dot).astype(LOW)
    ffn_out = einsum("the,hde->td", activated, down_full)
    ffn_dot = einsum("the,hde->td", act_dot, down_full) + einsum(
        "the,hde->td", activated, down_all[:, :, half:]
    )
    final_out, final_dot, normed_two, inverse_two = norm_pair(
        hidden + ffn_out,
        hidden_dot + ffn_dot,
        gain_anchor[2],
        bias_anchor[2],
        gain_delta[2],
        bias_delta[2],
    )

    def pooled(values):
        return (jnp.sum(jnp.where(live[:, None], values, 0.0), axis=0) / length_float).astype(LOW)

    feats = spread(jnp.concatenate([pooled(final_dot), pooled(final_out)])[None])
    feat_all = feats[:, D:]
    logits = einsum("gd,vd->gv", feat_all, table_anchor)
    logit_dot = einsum("gd,vd->gv", feats, both)
    vocab_iota = lax.broadcasted_iota(jnp.int32, logits.shape, 1)
    marks = [vocab_iota == labels[:, word : word + 1] for word in range(NLW)]
    peak_local = jnp.max(logits, axis=1)
    exponent = jnp.exp(logits - peak_local[:, None])
    stats = [peak_local, jnp.sum(exponent, axis=1), jnp.sum(exponent * logit_dot, axis=1)]
    stats += [jnp.sum(jnp.where(mark, logits, 0.0), axis=1) for mark in marks]
    stats += [jnp.sum(jnp.where(mark, logit_dot, 0.0), axis=1) for mark in marks]
    stats += [jnp.zeros_like(peak_local)] * (STATS - len(stats))
    stats = spread(jnp.stack(stats).reshape(1, STATS * count))
    coefficient, log_norm, loss_value = solve(stats, feat_all, targets_all)
    coefficient = coefficient.T
    grad_logits = -jnp.sum(coefficient, axis=1, keepdims=True) * jnp.exp(logits - log_norm.T)
    for word, mark in enumerate(marks):
        grad_logits = grad_logits + jnp.where(mark, coefficient[:, word : word + 1], 0.0)
    grad_logits = grad_logits.astype(LOW)
    grad_feat = einsum("gv,vd->gd", grad_logits, table_anchor)
    grad_feat = jnp.sum(lax.all_to_all(grad_feat, ALL, 0, 0, tiled=True), axis=0)

    grad_final = jnp.where(live[:, None], (grad_feat / length_float)[None, :], 0.0)
    grad_two, gain_two, bias_two_grad = norm_backward(
        grad_final, normed_two, inverse_two, gain_anchor[2]
    )

    def owned(gradient):
        low = gradient.astype(LOW).reshape(n_heads * D, -1)
        return lax.psum_scatter(low, ALL, scatter_dimension=0, tiled=True).astype(jnp.float32)

    grad_ffn = grad_two.astype(LOW)
    grad_down = owned(einsum("td,the->hde", grad_ffn, activated))
    grad_act = einsum("td,hde->the", grad_ffn, down_full)
    grad_pre = (slope * grad_act).astype(LOW)
    grad_up = owned(einsum("td,the->hde", ffn_input, grad_pre))
    grad_hidden = grad_two + einsum("the,hde->td", grad_pre, up_full)
    grad_one, gain_one, bias_one_grad = norm_backward(
        grad_hidden, normed_one, inverse_one, gain_anchor[1]
    )
    grad_attn = grad_one.astype(LOW)
    grad_out = einsum("td,the->hde", grad_attn, attended).astype(LOW)
    grad_att = einsum("td,hde->the", grad_attn, out_full).astype(LOW)
    grad_att = grad_att.reshape(SEQ, n_heads * local_heads, HDIM)
    grad_prob = einsum("qhd,khd->hqk", grad_att, value)
    grad_value = einsum("hqk,qhd->khd", probs_low, grad_att)
    delta_sum = jnp.sum(probs * grad_prob, axis=-1, keepdims=True)
    grad_score = (probs * (grad_prob - delta_sum)).astype(LOW)
    grad_query = einsum("hqk,khd->qhd", grad_score, key) * HDIM ** (-0.5)
    grad_key = einsum("hqk,qhd->khd", grad_score, query) * HDIM ** (-0.5)
    grad_rows = jnp.concatenate(
        [
            part.astype(LOW).reshape(SEQ, n_heads, group_wide)
            for part in (grad_query, grad_key, grad_value)
        ],
        axis=2,
    )
    grad_qkv = einsum("td,the->hde", attn_in, grad_rows).astype(LOW)
    grad_attn_all = owned(jnp.concatenate([grad_qkv, grad_out], axis=2))
    grad_start = grad_one + einsum("the,hde->td", grad_rows, attn_all[:, :, :three])
    grad_embed, gain_zero, bias_zero = norm_backward(
        grad_start, normed_zero, inverse_zero, gain_anchor[0]
    )
    grad_embed = grad_embed.astype(LOW)
    table_term = einsum("gv,gd->vd", grad_logits, feat_all) + give(0, wanted_first, grad_embed)
    table_grad = more(table_term, lambda turn: give(turn, asked(turn), grad_embed))

    gain_grad, bias_grad = total(
        (
            jnp.stack([gain_zero, gain_one, gain_two]),
            jnp.stack([bias_zero, bias_one_grad, bias_two_grad]),
        )
    )
    squares = sum(jnp.sum(part * part) for part in (table_grad, grad_attn_all, grad_up, grad_down))
    squares = total(squares.reshape(1, 1))[0, 0]
    squares = squares + jnp.sum(gain_grad * gain_grad) + jnp.sum(bias_grad * bias_grad)
    clip_scale = jnp.minimum(1.0, CLIP_NORM / jnp.sqrt(squares))
    steps_done = step_count[0].astype(jnp.float32)
    bias_one = 1.0 - jnp.power(BETA_ONE, steps_done)
    bias_two = 1.0 - jnp.power(BETA_TWO, steps_done)
    rates = (clip_scale, bias_one, bias_two)

    def with_out(qkv, out):
        return jnp.concatenate([qkv, out.T[None]], axis=0)

    height = qkv_delta.shape[1]
    turned = turned_update(
        soap_owners[0] == 1,
        with_out(qkv_delta, out_delta),
        jnp.swapaxes(grad_attn_all.reshape(height, 4, group_wide), 0, 1),
        with_out(qkv_first, out_first),
        with_out(qkv_second, out_second),
        soap_basis,
        *rates,
    )
    return (
        loss_value[0, 0],
        *adam_update(table_delta, table_grad, table_first, table_second, *rates),
        *(part[:3] for part in turned),
        *(part[3].T for part in turned),
        *adam_update(up_delta, grad_up, up_first, up_second, *rates),
        *adam_update(down_delta, grad_down.T, down_first, down_second, *rates),
        *adam_update(gain_delta, gain_grad, gain_first, gain_second, *rates),
        *adam_update(bias_delta, bias_grad, bias_first, bias_second, *rates),
    )


def solution(mesh):
    group = P("rows", None)
    table = P(("heads", "rows"), None)
    qkv = P(None, "rows", "heads")
    tall = P("heads", "rows")
    wide = P("rows", "heads")
    placed = (
        group,
        P("rows"),
        group,
        group,
        P(),
        P("rows"),
        P(None, "heads", None, None),
        *(table,) * 4,
        *(qkv,) * 4,
        *(tall,) * 4,
        *(wide,) * 4,
        *(tall,) * 4,
        *(P(),) * 8,
    )
    return jax.shard_map(
        per_device,
        mesh=mesh,
        in_specs=placed,
        out_specs=(
            P(),
            *(table,) * 3,
            *(qkv,) * 3,
            *(tall,) * 3,
            *(wide,) * 3,
            *(tall,) * 3,
            *(P(),) * 6,
        ),
        check_vma=False,
    )
```

```python
import jax
import jax.numpy as jnp
from jax import lax
from jax.experimental import pallas as pl
from jax.sharding import PartitionSpec as P

D = 768
HDIM = 64
SEQ = 256
NLW = 4
CGIT = 8
STATS = 16

EPS_NORM = 1e-05
BETA_ONE = 0.9
BETA_TWO = 0.999
ADAM_EPS = 1e-08
LEARN_RATE = 0.03
DECAY_RATE = 0.01
CLIP_NORM = 1.0
CG_SHIFT = 0.002
MASKED = -1e30
HALF_ROOT = 0.7071067811865476
INV_ROOT_TAU = 0.3989422804014327
HIGH = lax.Precision.HIGHEST
ALL = ("heads", "rows")
LOW = jnp.bfloat16


def einsum(form, left, right):
    return jnp.einsum(form, left, right, preferred_element_type=jnp.float32)


def gelu_slope(values):
    return (
        0.5 * (1.0 + lax.erf(values * HALF_ROOT))
        + values * jnp.exp(-0.5 * values * values) * INV_ROOT_TAU
    )


def norm_pair(values, dots, gain, bias, gain_dot, bias_dot):
    center = values - jnp.mean(values, axis=-1, keepdims=True)
    inverse = lax.rsqrt(jnp.mean(center * center, axis=-1, keepdims=True) + EPS_NORM)
    normed = center * inverse
    normed_dot = inverse * (
        dots
        - jnp.mean(dots, axis=-1, keepdims=True)
        - normed * jnp.mean(normed * dots, axis=-1, keepdims=True)
    )
    return (normed * gain + bias, normed_dot * gain + normed * gain_dot + bias_dot, normed, inverse)


def norm_backward(grad_out, normed, inverse, gain):
    scaled = grad_out * gain
    grad_in = inverse * (
        scaled
        - jnp.mean(scaled, axis=-1, keepdims=True)
        - normed * jnp.mean(scaled * normed, axis=-1, keepdims=True)
    )
    return (grad_in, jnp.sum(grad_out * normed, axis=0), jnp.sum(grad_out, axis=0))


def everyone(block):
    count = lax.axis_size(ALL[0]) * lax.axis_size(ALL[1])
    return lax.all_to_all(
        jnp.broadcast_to(block, (count, block.shape[1])), ALL, 0, 0, tiled=True
    )


def bits_of(axis):
    return [(axis, bit) for bit in reversed(range(lax.axis_size(axis).bit_length() - 1))]


def owned(parts):
    layout = [bit for axis in ALL for bit in bits_of(axis)]
    first = (ALL[0], 0)
    last = [bit for bit in layout if bit[0] == ALL[1] and bit[1] >= 2]
    middle = [bit for bit in layout if bit != first and bit not in last]
    results = []
    for turn, part in enumerate(parts):
        turn %= len(middle)
        order = [first] + middle[turn:] + middle[:turn] + last[::-1]
        left = list(layout)
        block = part.reshape((2,) * len(layout) + (-1, part.shape[-1]))
        for step in order:
            axis, bit = step
            place = left.index(step)
            mine = (lax.axis_index(axis) >> bit) & 1
            send = lax.dynamic_index_in_dim(block, 1 - mine, place, keepdims=False)
            keep = lax.dynamic_index_in_dim(block, mine, place, keepdims=False)
            size = lax.axis_size(axis)
            came = lax.ppermute(send, axis, [(index, index ^ (1 << bit)) for index in range(size)])
            block = keep.astype(jnp.float32) + came.astype(jnp.float32)
            left.pop(place)
            if left:
                block = block.astype(LOW)
        results.append(block)
    return results


def solve_kernel(stats_ref, feat_ref, targets_ref, coef_ref, norm_ref, loss_ref):
    count = feat_ref.shape[0]

    def stat(index):
        return stats_ref[:, index * count : (index + 1) * count]

    peaks = stat(0)
    peak = jnp.max(peaks, axis=0, keepdims=True)
    scale = jnp.exp(peaks - peak)
    mass = jnp.sum(stat(1) * scale, axis=0, keepdims=True)
    weighted = jnp.sum(stat(2) * scale, axis=0, keepdims=True)
    log_norm = peak + jnp.log(mass)
    shift = log_norm + weighted / mass
    picked = [
        jnp.sum(stat(3 + word) + stat(3 + NLW + word), axis=0, keepdims=True)
        for word in range(NLW)
    ]
    differ = jnp.concatenate(picked, axis=0) - shift - targets_ref[...]
    feat = feat_ref[...].astype(jnp.float32)
    center = feat - jnp.mean(feat, axis=0, keepdims=True)
    kernel = (
        lax.dot_general(
            center,
            center,
            (((1,), (1,)), ((), ())),
            precision=HIGH,
            preferred_element_type=jnp.float32,
        )
        / D
    )
    answer = jnp.zeros_like(differ)
    residual = differ
    direction = differ
    norm_now = jnp.sum(residual * residual, axis=1, keepdims=True)
    for step in range(CGIT):
        image = (
            jnp.dot(direction, kernel, precision=HIGH, preferred_element_type=jnp.float32)
            + CG_SHIFT * direction
        )
        alpha = norm_now / jnp.sum(direction * image, axis=1, keepdims=True)
        answer = answer + alpha * direction
        residual = residual - alpha * image
        if step + 1 < CGIT:
            norm_next = jnp.sum(residual * residual, axis=1, keepdims=True)
            direction = residual + norm_next / norm_now * direction
            norm_now = norm_next
    coef_ref[...] = 2.0 * answer / NLW
    norm_ref[...] = log_norm
    squares = jnp.sum(differ * differ, axis=1, keepdims=True)
    loss_ref[...] = jnp.sum(squares, axis=0, keepdims=True) / NLW


def solve(stats, feat, targets):
    count = feat.shape[0]
    return pl.pallas_call(
        solve_kernel,
        out_shape=(
            jax.ShapeDtypeStruct((NLW, count), jnp.float32),
            jax.ShapeDtypeStruct((1, count), jnp.float32),
            jax.ShapeDtypeStruct((1, 1), jnp.float32),
        ),
    )(stats, feat, targets)


def adam_moments(gradient, moment_one, moment_two, bias_one, bias_two):
    new_one = BETA_ONE * moment_one + (1.0 - BETA_ONE) * gradient
    new_two = BETA_TWO * moment_two + (1.0 - BETA_TWO) * gradient * gradient
    return (new_one / bias_one / (jnp.sqrt(new_two / bias_two) + ADAM_EPS), new_one, new_two)


def adam_update(master, gradient, moment_one, moment_two, clip_scale, bias_one, bias_two):
    direction, new_one, new_two = adam_moments(
        clip_scale * gradient, moment_one, moment_two, bias_one, bias_two
    )
    return (master - LEARN_RATE * (direction + DECAY_RATE * master), new_one, new_two)


def turned_update(owner, master, gradient, first, second, basis, clip_scale, bias_one, bias_two):
    count, height, width = gradient.shape

    def grouped(array):
        return array.reshape(count, height, width // HDIM, HDIM)

    plain = clip_scale * gradient
    turned = jnp.einsum("ciha,chab->cihb", grouped(plain), basis, precision=HIGH)
    used = jnp.where(owner, turned.reshape(gradient.shape), plain)
    direction, new_one, new_two = adam_moments(used, first, second, bias_one, bias_two)
    back = jnp.einsum("cihb,chab->ciha", grouped(direction), basis, precision=HIGH)
    direction = jnp.where(owner, back.reshape(gradient.shape), direction)
    return (master - LEARN_RATE * (direction + DECAY_RATE * master), new_one, new_two)


def per_device(
    token_ids,
    lengths,
    label_ids,
    targets,
    step_count,
    soap_owners,
    soap_basis,
    table_anchor,
    table_delta,
    table_first,
    table_second,
    qkv_anchor,
    qkv_delta,
    qkv_first,
    qkv_second,
    out_anchor,
    out_delta,
    out_first,
    out_second,
    up_anchor,
    up_delta,
    up_first,
    up_second,
    down_anchor,
    down_delta,
    down_first,
    down_second,
    gain_anchor,
    gain_delta,
    gain_first,
    gain_second,
    bias_anchor,
    bias_delta,
    bias_first,
    bias_second,
):
    n_heads = lax.axis_size("heads")
    n_rows = lax.axis_size("rows")
    count = n_heads * n_rows
    head_index = lax.axis_index("heads")
    me = head_index * n_rows + lax.axis_index("rows")
    vocab = table_anchor.shape[0]
    group_wide = qkv_anchor.shape[2]
    local_heads = group_wide // HDIM

    def side_by_side(qkv, out):
        return jnp.concatenate([qkv[0], qkv[1], qkv[2], out.T], axis=1)

    def gathered(anchor, delta):
        block = jnp.concatenate([anchor, delta.astype(LOW)], axis=1)
        full = lax.all_gather(block, ALL, axis=0, tiled=True)
        return full.reshape(n_heads, D, block.shape[1])

    attn_all = gathered(side_by_side(qkv_anchor, out_anchor), side_by_side(qkv_delta, out_delta))
    ffn_all = gathered(
        jnp.concatenate([up_anchor, down_anchor.T], axis=1),
        jnp.concatenate([up_delta, down_delta.T], axis=1),
    )

    room = 8 * -(-(2 * SEQ // count + 8) // 8)
    slots = count * room
    ids = lax.dynamic_index_in_dim(token_ids, head_index, 0, keepdims=False)
    owner = ids // vocab
    local = ids - owner * vocab
    place = lax.iota(jnp.int32, SEQ)
    same = ids[:, None] == ids[None, :]
    earliest = jnp.min(jnp.where(same, place[None, :], SEQ), axis=1)
    leads = earliest == place
    rank = jnp.sum(
        (leads[None, :] & (owner[:, None] == owner[None, :]) & (place[None, :] < earliest[:, None])),
        axis=1,
        dtype=jnp.int32,
    )
    longest = jnp.max(rank) + 1
    own_labels = lax.dynamic_index_in_dim(label_ids, head_index, 0, keepdims=False)
    own_targets = lax.dynamic_index_in_dim(targets, head_index, 0, keepdims=False)
    notes = jnp.concatenate(
        [longest[None].astype(jnp.float32), own_labels.astype(jnp.float32), own_targets]
    )
    both = jnp.concatenate([table_anchor, table_delta.astype(LOW)], axis=1)

    def slot_of(turn):
        within = rank - turn * room
        return jnp.where((within >= 0) & (within < room), owner * room + within, -1)

    def wanted_of(turn):
        taken = jnp.where(leads, slot_of(turn), -1)
        hit = lax.iota(jnp.int32, slots)[:, None] == taken[None, :]
        return (jnp.sum(jnp.where(hit, local[None, :] + 1, 0), axis=1) - 1).reshape(count, room)

    def asked(turn):
        return lax.all_to_all(wanted_of(turn), ALL, 0, 0, tiled=True).reshape(slots)

    def chosen(wanted):
        return (wanted[:, None] == lax.broadcasted_iota(jnp.int32, (slots, vocab), 1)).astype(LOW)

    def token_slots(turn):
        return (
            slot_of(turn)[:, None] == lax.broadcasted_iota(jnp.int32, (SEQ, slots), 1)
        ).astype(LOW)

    def fetch(turn, wanted):
        rows = einsum("sv,vd->sd", chosen(wanted), both).astype(LOW)
        rows = lax.all_to_all(rows.reshape(count, room, 2 * D), ALL, 0, 0, tiled=True)
        return einsum("ts,sd->td", token_slots(turn), rows.reshape(slots, 2 * D))

    def give(turn, wanted, grads):
        sums = einsum("ts,td->sd", token_slots(turn), grads).astype(LOW)
        sums = lax.all_to_all(sums.reshape(count, room, D), ALL, 0, 0, tiled=True)
        return einsum("sv,sd->vd", chosen(wanted), sums.reshape(slots, D))

    def more(start, step):
        def rest(value):
            return lax.fori_loop(1, rounds, lambda turn, so_far: so_far + step(turn), value)

        return lax.cond(rounds > 1, rest, lambda value: value, start)

    message = jnp.concatenate(
        [
            wanted_of(0).astype(jnp.float32),
            jnp.broadcast_to(notes[None], (count, notes.shape[0])),
        ],
        axis=1,
    )
    message = lax.all_to_all(message, ALL, 0, 0, tiled=True)
    wanted_first = message[:, :room].astype(jnp.int32).reshape(slots)
    rounds = -(-jnp.max(message[:, room]).astype(jnp.int32) // room)
    labels = message[:, room + 1 : room + 1 + NLW].astype(jnp.int32) - me * vocab
    targets_all = message[:, room + 1 + NLW :].T
    embedded_both = more(fetch(0, wanted_first), lambda turn: fetch(turn, asked(turn)))
    start_x, start_dot, normed_zero, inverse_zero = norm_pair(
        embedded_both[:, :D],
        embedded_both[:, D:],
        gain_anchor[0],
        bias_anchor[0],
        gain_delta[0],
        bias_delta[0],
    )

    own_length = lax.dynamic_index_in_dim(lengths, head_index, 0, keepdims=False)
    live = lax.iota(jnp.int32, SEQ) < own_length
    length_float = own_length.astype(jnp.float32)

    attn_in = start_x.astype(LOW)
    attn_dot_in = start_dot.astype(LOW)
    three = 3 * group_wide
    wide = attn_all.shape[2] // 2
    through = einsum("td,hde->the", attn_in, attn_all)
    projected = through[:, :, :three].astype(LOW)
    projected_dot = (
        through[:, :, wide : wide + three]
        + einsum("td,hde->the", attn_dot_in, attn_all[:, :, :three])
    ).astype(LOW)

    def split_heads(array):
        array = array.reshape(SEQ, n_heads, 3, local_heads, HDIM)
        return [array[:, :, index].reshape(SEQ, n_heads * local_heads, HDIM) for index in range(3)]

    query, key, value = split_heads(projected)
    query_dot, key_dot, value_dot = split_heads(projected_dot)
    scores = einsum("qhd,khd->hqk", query, key) * HDIM ** (-0.5)
    scores = jnp.where(live[None, None, :], scores, MASKED)
    exponent = jnp.exp(scores - jnp.max(scores, axis=-1, keepdims=True))
    probs = exponent / jnp.sum(exponent, axis=-1, keepdims=True)
    probs_low = probs.astype(LOW)
    score_dot = (
        einsum("qhd,khd->hqk", query_dot, key) + einsum("qhd,khd->hqk", query, key_dot)
    ) * HDIM ** (-0.5)
    prob_dot = (probs * (score_dot - jnp.sum(probs * score_dot, axis=-1, keepdims=True))).astype(LOW)
    attended = einsum("hqk,khd->qhd", probs_low, value).astype(LOW)
    attended_dot = (
        einsum("hqk,khd->qhd", prob_dot, value) + einsum("hqk,khd->qhd", probs_low, value_dot)
    ).astype(LOW)
    attended = attended.reshape(SEQ, n_heads, group_wide)
    attended_dot = attended_dot.reshape(SEQ, n_heads, group_wide)
    out_full = attn_all[:, :, three:wide]
    out_step = attn_all[:, :, wide + three :]
    attn_out = einsum("the,hde->td", attended, out_full)
    attn_dot = einsum("the,hde->td", attended_dot, out_full) + einsum(
        "the,hde->td", attended, out_step
    )
    hidden, hidden_dot, normed_one, inverse_one = norm_pair(
        start_x + attn_out,
        start_dot + attn_dot,
        gain_anchor[1],
        bias_anchor[1],
        gain_delta[1],
        bias_delta[1],
    )
    ffn_input = hidden.astype(LOW)
    up_full, down_full, up_step, down_step = jnp.split(ffn_all, 4, axis=2)
    pre_gelu = einsum("td,hde->the", ffn_input, up_full)
    pre_dot = einsum("td,hde->the", hidden_dot.astype(LOW), up_full) + einsum(
        "td,hde->the", ffn_input, up_step
    )
    activated = jax.nn.gelu(pre_gelu, approximate=False).astype(LOW)
    slope = gelu_slope(pre_gelu)
    act_dot = (slope * pre_dot).astype(LOW)
    ffn_out = einsum("the,hde->td", activated, down_full)
    ffn_dot = einsum("the,hde->td", act_dot, down_full) + einsum(
        "the,hde->td", activated, down_step
    )
    final_out, final_dot, normed_two, inverse_two = norm_pair(
        hidden + ffn_out,
        hidden_dot + ffn_dot,
        gain_anchor[2],
        bias_anchor[2],
        gain_delta[2],
        bias_delta[2],
    )

    def pooled(values):
        return (jnp.sum(jnp.where(live[:, None], values, 0.0), axis=0) / length_float).astype(LOW)

    feats = everyone(jnp.concatenate([pooled(final_dot), pooled(final_out)])[None])
    feat_all = feats[:, D:]
    logits = einsum("gd,vd->gv", feat_all, table_anchor)
    logit_dot = einsum("gd,vd->gv", feats, both)
    vocab_iota = lax.broadcasted_iota(jnp.int32, logits.shape, 1)
    marks = [vocab_iota == labels[:, word : word + 1] for word in range(NLW)]
    peak_local = jnp.max(logits, axis=1)
    exponent = jnp.exp(logits - peak_local[:, None])
    stats = [peak_local, jnp.sum(exponent, axis=1), jnp.sum(exponent * logit_dot, axis=1)]
    stats += [jnp.sum(jnp.where(mark, logits, 0.0), axis=1) for mark in marks]
    stats += [jnp.sum(jnp.where(mark, logit_dot, 0.0), axis=1) for mark in marks]
    stats += [jnp.zeros_like(peak_local)] * (STATS - len(stats))
    stats = everyone(jnp.stack(stats).reshape(1, STATS * count))
    coefficient, log_norm, loss_value = solve(stats, feat_all, targets_all)
    coefficient = coefficient.T
    grad_logits = -jnp.sum(coefficient, axis=1, keepdims=True) * jnp.exp(logits - log_norm.T)
    for word, mark in enumerate(marks):
        grad_logits = grad_logits + jnp.where(mark, coefficient[:, word : word + 1], 0.0)
    grad_logits = grad_logits.astype(LOW)
    grad_feat = einsum("gv,vd->gd", grad_logits, table_anchor)
    grad_feat = jnp.sum(lax.all_to_all(grad_feat, ALL, 0, 0, tiled=True), axis=0)

    grad_final = jnp.where(live[:, None], (grad_feat / length_float)[None, :], 0.0)
    grad_two, gain_two, bias_two_grad = norm_backward(
        grad_final, normed_two, inverse_two, gain_anchor[2]
    )

    grad_ffn = grad_two.astype(LOW)
    grad_down = einsum("td,the->hde", grad_ffn, activated).astype(LOW)
    grad_act = einsum("td,hde->the", grad_ffn, down_full)
    grad_pre = (slope * grad_act).astype(LOW)
    grad_up = einsum("td,the->hde", ffn_input, grad_pre).astype(LOW)
    grad_hidden = grad_two + einsum("the,hde->td", grad_pre, up_full)
    grad_one, gain_one, bias_one_grad = norm_backward(
        grad_hidden, normed_one, inverse_one, gain_anchor[1]
    )
    grad_attn = grad_one.astype(LOW)
    grad_out = einsum("td,the->hde", grad_attn, attended).astype(LOW)
    grad_att = einsum("td,hde->the", grad_attn, out_full).astype(LOW)
    grad_att = grad_att.reshape(SEQ, n_heads * local_heads, HDIM)
    grad_prob = einsum("qhd,khd->hqk", grad_att, value)
    grad_value = einsum("hqk,qhd->khd", probs_low, grad_att)
    delta_sum = jnp.sum(probs * grad_prob, axis=-1, keepdims=True)
    grad_score = (probs * (grad_prob - delta_sum)).astype(LOW)
    grad_query = einsum("hqk,khd->qhd", grad_score, key) * HDIM ** (-0.5)
    grad_key = einsum("hqk,qhd->khd", grad_score, query) * HDIM ** (-0.5)
    grad_rows = jnp.concatenate(
        [
            part.astype(LOW).reshape(SEQ, n_heads, group_wide)
            for part in (grad_query, grad_key, grad_value)
        ],
        axis=2,
    )
    grad_qkv = einsum("td,the->hde", attn_in, grad_rows).astype(LOW)
    grad_attn_all = jnp.concatenate([grad_qkv, grad_out], axis=2)
    grad_down, grad_up, grad_attn_all = owned([grad_down, grad_up, grad_attn_all])
    grad_start = grad_one + einsum("the,hde->td", grad_rows, attn_all[:, :, :three])
    grad_embed, gain_zero, bias_zero = norm_backward(
        grad_start, normed_zero, inverse_zero, gain_anchor[0]
    )
    grad_embed = grad_embed.astype(LOW)
    table_term = einsum("gv,gd->vd", grad_logits, feat_all) + give(0, wanted_first, grad_embed)
    table_grad = more(table_term, lambda turn: give(turn, asked(turn), grad_embed))

    norm_grads = jnp.stack(
        [gain_zero, gain_one, gain_two, bias_zero, bias_one_grad, bias_two_grad]
    )
    pieces = lax.all_to_all(norm_grads.reshape(count, -1), ALL, 0, 0, tiled=True)
    piece = jnp.sum(pieces, axis=0, keepdims=True)
    gain_grad, bias_grad = everyone(piece).reshape(2, 3, D)
    squares = sum(
        jnp.sum(part * part) for part in (table_grad, grad_attn_all, grad_up, grad_down, piece)
    )
    squares = jnp.sum(everyone(jnp.broadcast_to(squares, (1, 128)))[:, 0])
    clip_scale = jnp.minimum(1.0, CLIP_NORM / jnp.sqrt(squares))
    steps_done = step_count[0].astype(jnp.float32)
    bias_one = 1.0 - jnp.power(BETA_ONE, steps_done)
    bias_two = 1.0 - jnp.power(BETA_TWO, steps_done)
    rates = (clip_scale, bias_one, bias_two)

    def with_out(qkv, out):
        return jnp.concatenate([qkv, out.T[None]], axis=0)

    height = qkv_delta.shape[1]
    turned = turned_update(
        soap_owners[0] == 1,
        with_out(qkv_delta, out_delta),
        jnp.swapaxes(grad_attn_all.reshape(height, 4, group_wide), 0, 1),
        with_out(qkv_first, out_first),
        with_out(qkv_second, out_second),
        soap_basis,
        *rates,
    )
    return (
        loss_value[0, 0],
        *adam_update(table_delta, table_grad, table_first, table_second, *rates),
        *(part[:3] for part in turned),
        *(part[3].T for part in turned),
        *adam_update(up_delta, grad_up, up_first, up_second, *rates),
        *adam_update(down_delta, grad_down.T, down_first, down_second, *rates),
        *adam_update(gain_delta, gain_grad, gain_first, gain_second, *rates),
        *adam_update(bias_delta, bias_grad, bias_first, bias_second, *rates),
    )


def solution(mesh):
    group = P("rows", None)
    table = P(("heads", "rows"), None)
    qkv = P(None, "rows", "heads")
    tall = P("heads", "rows")
    wide = P("rows", "heads")
    placed = (
        group,
        P("rows"),
        group,
        group,
        P(),
        P("rows"),
        P(None, "heads", None, None),
        *(table,) * 4,
        *(qkv,) * 4,
        *(tall,) * 4,
        *(wide,) * 4,
        *(tall,) * 4,
        *(P(),) * 8,
    )
    return jax.shard_map(
        per_device,
        mesh=mesh,
        in_specs=placed,
        out_specs=(
            P(),
            *(table,) * 3,
            *(qkv,) * 3,
            *(tall,) * 3,
            *(wide,) * 3,
            *(tall,) * 3,
            *(P(),) * 6,
        ),
        check_vma=False,
    )
```

```python
import jax
import jax.numpy as jnp
from jax import lax
from jax.experimental import pallas as pl
from jax.sharding import PartitionSpec as P

D = 768
HDIM = 64
SEQ = 256
NLW = 4
CGIT = 8
STATS = 16

EPS_NORM = 1e-05
BETA_ONE = 0.9
BETA_TWO = 0.999
ADAM_EPS = 1e-08
LEARN_RATE = 0.03
DECAY_RATE = 0.01
CLIP_NORM = 1.0
CG_SHIFT = 0.002
MASKED = -1e30
HALF_ROOT = 0.7071067811865476
INV_ROOT_TAU = 0.3989422804014327
HIGH = lax.Precision.HIGHEST
ALL = ("heads", "rows")
LOW = jnp.bfloat16


def einsum(form, left, right):
    return jnp.einsum(form, left, right, preferred_element_type=jnp.float32)


def gelu_slope(values):
    return (
        0.5 * (1.0 + lax.erf(values * HALF_ROOT))
        + values * jnp.exp(-0.5 * values * values) * INV_ROOT_TAU
    )


def norm_pair(values, dots, gain, bias, gain_dot, bias_dot):
    center = values - jnp.mean(values, axis=-1, keepdims=True)
    inverse = lax.rsqrt(jnp.mean(center * center, axis=-1, keepdims=True) + EPS_NORM)
    normed = center * inverse
    normed_dot = inverse * (
        dots
        - jnp.mean(dots, axis=-1, keepdims=True)
        - normed * jnp.mean(normed * dots, axis=-1, keepdims=True)
    )
    return (normed * gain + bias, normed_dot * gain + normed * gain_dot + bias_dot, normed, inverse)


def norm_backward(grad_out, normed, inverse, gain):
    scaled = grad_out * gain
    grad_in = inverse * (
        scaled
        - jnp.mean(scaled, axis=-1, keepdims=True)
        - normed * jnp.mean(scaled * normed, axis=-1, keepdims=True)
    )
    return (grad_in, jnp.sum(grad_out * normed, axis=0), jnp.sum(grad_out, axis=0))


def everyone(block):
    count = lax.axis_size(ALL[0]) * lax.axis_size(ALL[1])
    return lax.all_to_all(
        jnp.broadcast_to(block, (count, block.shape[1])), ALL, 0, 0, tiled=True
    )


def bits_of(axis):
    return [(axis, bit) for bit in reversed(range(lax.axis_size(axis).bit_length() - 1))]


def plan():
    layout = [bit for axis in ALL for bit in bits_of(axis)]
    first = (ALL[0], 0)
    last = [bit for bit in layout if bit[0] == ALL[1] and bit[1] >= 2]
    middle = [bit for bit in layout if bit != first and bit not in last]
    return layout, first, middle, last


def swapped(block, step):
    axis, bit = step
    size = lax.axis_size(axis)
    return lax.ppermute(block, axis, [(index, index ^ (1 << bit)) for index in range(size)])


def assembled(blocks):
    layout, first, middle, last = plan()
    turns = ((1, 0, 2), (0, 2, 1), (2, 1, 0))
    results = []
    for block, turn in zip(blocks, turns):
        shape = block.shape
        have = []
        for step in last + [middle[index] for index in turn] + [first]:
            axis, bit = step
            came = swapped(block, step)
            have = [other for other in layout if other in have or other == step]
            place = have.index(step)
            joined = jnp.stack([block, came], axis=place)
            if axis != ALL[0]:
                upper = ((lax.axis_index(axis) >> bit) & 1) > 0
                joined = jnp.where(upper, jnp.stack([came, block], axis=place), joined)
            block = joined
        results.append(block.reshape(lax.axis_size(ALL[0]), -1, shape[1]))
    return results


def owned(parts):
    layout, first, middle, last = plan()
    results = []
    for turn, part in enumerate(parts):
        turn %= len(middle)
        order = [first] + middle[turn:] + middle[:turn] + last[::-1]
        left = list(layout)
        block = part.reshape((2,) * len(layout) + (-1, part.shape[-1]))
        for step in order:
            axis, bit = step
            place = left.index(step)
            if axis == ALL[0]:
                keep = lax.index_in_dim(block, 0, place, keepdims=False)
                send = lax.index_in_dim(block, 1, place, keepdims=False)
            else:
                mine = (lax.axis_index(axis) >> bit) & 1
                keep = lax.dynamic_index_in_dim(block, mine, place, keepdims=False)
                send = lax.dynamic_index_in_dim(block, 1 - mine, place, keepdims=False)
            block = keep.astype(jnp.float32) + swapped(send, step).astype(jnp.float32)
            left.pop(place)
            if left:
                block = block.astype(LOW)
        results.append(block)
    return results


def solve_kernel(stats_ref, feat_ref, targets_ref, coef_ref, norm_ref, loss_ref):
    count = feat_ref.shape[0]

    def stat(index):
        return stats_ref[:, index * count : (index + 1) * count]

    peaks = stat(0)
    peak = jnp.max(peaks, axis=0, keepdims=True)
    scale = jnp.exp(peaks - peak)
    mass = jnp.sum(stat(1) * scale, axis=0, keepdims=True)
    weighted = jnp.sum(stat(2) * scale, axis=0, keepdims=True)
    log_norm = peak + jnp.log(mass)
    shift = log_norm + weighted / mass
    picked = [
        jnp.sum(stat(3 + word) + stat(3 + NLW + word), axis=0, keepdims=True)
        for word in range(NLW)
    ]
    differ = jnp.concatenate(picked, axis=0) - shift - targets_ref[...]
    feat = feat_ref[...].astype(jnp.float32)
    center = feat - jnp.mean(feat, axis=0, keepdims=True)
    kernel = (
        lax.dot_general(
            center,
            center,
            (((1,), (1,)), ((), ())),
            precision=HIGH,
            preferred_element_type=jnp.float32,
        )
        / D
    )
    answer = jnp.zeros_like(differ)
    residual = differ
    direction = differ
    norm_now = jnp.sum(residual * residual, axis=1, keepdims=True)
    for step in range(CGIT):
        image = (
            jnp.dot(direction, kernel, precision=HIGH, preferred_element_type=jnp.float32)
            + CG_SHIFT * direction
        )
        alpha = norm_now / jnp.sum(direction * image, axis=1, keepdims=True)
        answer = answer + alpha * direction
        residual = residual - alpha * image
        if step + 1 < CGIT:
            norm_next = jnp.sum(residual * residual, axis=1, keepdims=True)
            direction = residual + norm_next / norm_now * direction
            norm_now = norm_next
    coef_ref[...] = 2.0 * answer / NLW
    norm_ref[...] = log_norm
    squares = jnp.sum(differ * differ, axis=1, keepdims=True)
    loss_ref[...] = jnp.sum(squares, axis=0, keepdims=True) / NLW


def solve(stats, feat, targets):
    count = feat.shape[0]
    return pl.pallas_call(
        solve_kernel,
        out_shape=(
            jax.ShapeDtypeStruct((NLW, count), jnp.float32),
            jax.ShapeDtypeStruct((1, count), jnp.float32),
            jax.ShapeDtypeStruct((1, 1), jnp.float32),
        ),
    )(stats, feat, targets)


def adam_moments(gradient, moment_one, moment_two, bias_one, bias_two):
    new_one = BETA_ONE * moment_one + (1.0 - BETA_ONE) * gradient
    new_two = BETA_TWO * moment_two + (1.0 - BETA_TWO) * gradient * gradient
    return (new_one / bias_one / (jnp.sqrt(new_two / bias_two) + ADAM_EPS), new_one, new_two)


def adam_update(master, gradient, moment_one, moment_two, clip_scale, bias_one, bias_two):
    direction, new_one, new_two = adam_moments(
        clip_scale * gradient, moment_one, moment_two, bias_one, bias_two
    )
    return (master - LEARN_RATE * (direction + DECAY_RATE * master), new_one, new_two)


def turned_update(owner, master, gradient, first, second, basis, clip_scale, bias_one, bias_two):
    count, height, width = gradient.shape

    def grouped(array):
        return array.reshape(count, height, width // HDIM, HDIM)

    plain = clip_scale * gradient
    turned = jnp.einsum("ciha,chab->cihb", grouped(plain), basis, precision=HIGH)
    used = jnp.where(owner, turned.reshape(gradient.shape), plain)
    direction, new_one, new_two = adam_moments(used, first, second, bias_one, bias_two)
    back = jnp.einsum("cihb,chab->ciha", grouped(direction), basis, precision=HIGH)
    direction = jnp.where(owner, back.reshape(gradient.shape), direction)
    return (master - LEARN_RATE * (direction + DECAY_RATE * master), new_one, new_two)


def per_device(
    token_ids,
    lengths,
    label_ids,
    targets,
    step_count,
    soap_owners,
    soap_basis,
    table_anchor,
    table_delta,
    table_first,
    table_second,
    qkv_anchor,
    qkv_delta,
    qkv_first,
    qkv_second,
    out_anchor,
    out_delta,
    out_first,
    out_second,
    up_anchor,
    up_delta,
    up_first,
    up_second,
    down_anchor,
    down_delta,
    down_first,
    down_second,
    gain_anchor,
    gain_delta,
    gain_first,
    gain_second,
    bias_anchor,
    bias_delta,
    bias_first,
    bias_second,
):
    n_heads = lax.axis_size("heads")
    n_rows = lax.axis_size("rows")
    count = n_heads * n_rows
    head_index = lax.axis_index("heads")
    me = head_index * n_rows + lax.axis_index("rows")
    vocab = table_anchor.shape[0]
    group_wide = qkv_anchor.shape[2]
    local_heads = group_wide // HDIM

    def side_by_side(qkv, out):
        return jnp.concatenate([qkv[0], qkv[1], qkv[2], out.T], axis=1)

    def packed(anchor, delta):
        return jnp.concatenate([anchor, delta.astype(LOW)], axis=1)

    attn_all, up_all, down_all = assembled(
        [
            packed(side_by_side(qkv_anchor, out_anchor), side_by_side(qkv_delta, out_delta)),
            packed(up_anchor, up_delta),
            packed(down_anchor.T, down_delta.T),
        ]
    )

    room = 8 * -(-(2 * SEQ // count + 8) // 8)
    slots = count * room
    ids = lax.dynamic_index_in_dim(token_ids, head_index, 0, keepdims=False)
    owner = ids // vocab
    local = ids - owner * vocab
    place = lax.iota(jnp.int32, SEQ)
    same = ids[:, None] == ids[None, :]
    earliest = jnp.min(jnp.where(same, place[None, :], SEQ), axis=1)
    leads = earliest == place
    rank = jnp.sum(
        (leads[None, :] & (owner[:, None] == owner[None, :]) & (place[None, :] < earliest[:, None])),
        axis=1,
        dtype=jnp.int32,
    )
    longest = jnp.max(rank) + 1
    own_labels = lax.dynamic_index_in_dim(label_ids, head_index, 0, keepdims=False)
    own_targets = lax.dynamic_index_in_dim(targets, head_index, 0, keepdims=False)
    notes = jnp.concatenate(
        [longest[None].astype(jnp.float32), own_labels.astype(jnp.float32), own_targets]
    )
    both = jnp.concatenate([table_anchor, table_delta.astype(LOW)], axis=1)

    def slot_of(turn):
        within = rank - turn * room
        return jnp.where((within >= 0) & (within < room), owner * room + within, -1)

    def wanted_of(turn):
        taken = jnp.where(leads, slot_of(turn), -1)
        hit = lax.iota(jnp.int32, slots)[:, None] == taken[None, :]
        return (jnp.sum(jnp.where(hit, local[None, :] + 1, 0), axis=1) - 1).reshape(count, room)

    def asked(turn):
        return lax.all_to_all(wanted_of(turn), ALL, 0, 0, tiled=True).reshape(slots)

    def chosen(wanted):
        return (wanted[:, None] == lax.broadcasted_iota(jnp.int32, (slots, vocab), 1)).astype(LOW)

    def token_slots(turn):
        return (
            slot_of(turn)[:, None] == lax.broadcasted_iota(jnp.int32, (SEQ, slots), 1)
        ).astype(LOW)

    def fetch(turn, wanted):
        rows = einsum("sv,vd->sd", chosen(wanted), both).astype(LOW)
        rows = lax.all_to_all(rows.reshape(count, room, 2 * D), ALL, 0, 0, tiled=True)
        return einsum("ts,sd->td", token_slots(turn), rows.reshape(slots, 2 * D))

    def give(turn, wanted, grads):
        sums = einsum("ts,td->sd", token_slots(turn), grads).astype(LOW)
        sums = lax.all_to_all(sums.reshape(count, room, D), ALL, 0, 0, tiled=True)
        return einsum("sv,sd->vd", chosen(wanted), sums.reshape(slots, D))

    def more(start, step):
        def rest(value):
            return lax.fori_loop(1, rounds, lambda turn, so_far: so_far + step(turn), value)

        return lax.cond(rounds > 1, rest, lambda value: value, start)

    message = jnp.concatenate(
        [
            wanted_of(0).astype(jnp.float32),
            jnp.broadcast_to(notes[None], (count, notes.shape[0])),
        ],
        axis=1,
    )
    message = lax.all_to_all(message, ALL, 0, 0, tiled=True)
    wanted_first = message[:, :room].astype(jnp.int32).reshape(slots)
    rounds = -(-jnp.max(message[:, room]).astype(jnp.int32) // room)
    labels = message[:, room + 1 : room + 1 + NLW].astype(jnp.int32) - me * vocab
    targets_all = message[:, room + 1 + NLW :].T
    embedded_both = more(fetch(0, wanted_first), lambda turn: fetch(turn, asked(turn)))
    start_x, start_dot, normed_zero, inverse_zero = norm_pair(
        embedded_both[:, :D],
        embedded_both[:, D:],
        gain_anchor[0],
        bias_anchor[0],
        gain_delta[0],
        bias_delta[0],
    )

    own_length = lax.dynamic_index_in_dim(lengths, head_index, 0, keepdims=False)
    live = lax.iota(jnp.int32, SEQ) < own_length
    length_float = own_length.astype(jnp.float32)

    attn_in = start_x.astype(LOW)
    attn_dot_in = start_dot.astype(LOW)
    three = 3 * group_wide
    wide = attn_all.shape[2] // 2
    through = einsum("td,hde->the", attn_in, attn_all)
    projected = through[:, :, :three].astype(LOW)
    projected_dot = (
        through[:, :, wide : wide + three]
        + einsum("td,hde->the", attn_dot_in, attn_all[:, :, :three])
    ).astype(LOW)

    def split_heads(array):
        array = array.reshape(SEQ, n_heads, 3, local_heads, HDIM)
        return [array[:, :, index].reshape(SEQ, n_heads * local_heads, HDIM) for index in range(3)]

    query, key, value = split_heads(projected)
    query_dot, key_dot, value_dot = split_heads(projected_dot)
    scores = einsum("qhd,khd->hqk", query, key) * HDIM ** (-0.5)
    scores = jnp.where(live[None, None, :], scores, MASKED)
    exponent = jnp.exp(scores - jnp.max(scores, axis=-1, keepdims=True))
    probs = exponent / jnp.sum(exponent, axis=-1, keepdims=True)
    probs_low = probs.astype(LOW)
    score_dot = (
        einsum("qhd,khd->hqk", query_dot, key) + einsum("qhd,khd->hqk", query, key_dot)
    ) * HDIM ** (-0.5)
    prob_dot = (probs * (score_dot - jnp.sum(probs * score_dot, axis=-1, keepdims=True))).astype(LOW)
    attended = einsum("hqk,khd->qhd", probs_low, value).astype(LOW)
    attended_dot = (
        einsum("hqk,khd->qhd", prob_dot, value) + einsum("hqk,khd->qhd", probs_low, value_dot)
    ).astype(LOW)
    attended = attended.reshape(SEQ, n_heads, group_wide)
    attended_dot = attended_dot.reshape(SEQ, n_heads, group_wide)
    out_full = attn_all[:, :, three:wide]
    out_step = attn_all[:, :, wide + three :]
    attn_out = einsum("the,hde->td", attended, out_full)
    attn_dot = einsum("the,hde->td", attended_dot, out_full) + einsum(
        "the,hde->td", attended, out_step
    )
    hidden, hidden_dot, normed_one, inverse_one = norm_pair(
        start_x + attn_out,
        start_dot + attn_dot,
        gain_anchor[1],
        bias_anchor[1],
        gain_delta[1],
        bias_delta[1],
    )
    ffn_input = hidden.astype(LOW)
    up_full, up_step = jnp.split(up_all, 2, axis=2)
    down_full, down_step = jnp.split(down_all, 2, axis=2)
    pre_gelu = einsum("td,hde->the", ffn_input, up_full)
    pre_dot = einsum("td,hde->the", hidden_dot.astype(LOW), up_full) + einsum(
        "td,hde->the", ffn_input, up_step
    )
    activated = jax.nn.gelu(pre_gelu, approximate=False).astype(LOW)
    slope = gelu_slope(pre_gelu)
    act_dot = (slope * pre_dot).astype(LOW)
    ffn_out = einsum("the,hde->td", activated, down_full)
    ffn_dot = einsum("the,hde->td", act_dot, down_full) + einsum(
        "the,hde->td", activated, down_step
    )
    final_out, final_dot, normed_two, inverse_two = norm_pair(
        hidden + ffn_out,
        hidden_dot + ffn_dot,
        gain_anchor[2],
        bias_anchor[2],
        gain_delta[2],
        bias_delta[2],
    )

    def pooled(values):
        return (jnp.sum(jnp.where(live[:, None], values, 0.0), axis=0) / length_float).astype(LOW)

    feats = everyone(jnp.concatenate([pooled(final_dot), pooled(final_out)])[None])
    feat_all = feats[:, D:]
    logits = einsum("gd,vd->gv", feat_all, table_anchor)
    logit_dot = einsum("gd,vd->gv", feats, both)
    vocab_iota = lax.broadcasted_iota(jnp.int32, logits.shape, 1)
    marks = [vocab_iota == labels[:, word : word + 1] for word in range(NLW)]
    peak_local = jnp.max(logits, axis=1)
    exponent = jnp.exp(logits - peak_local[:, None])
    stats = [peak_local, jnp.sum(exponent, axis=1), jnp.sum(exponent * logit_dot, axis=1)]
    stats += [jnp.sum(jnp.where(mark, logits, 0.0), axis=1) for mark in marks]
    stats += [jnp.sum(jnp.where(mark, logit_dot, 0.0), axis=1) for mark in marks]
    stats += [jnp.zeros_like(peak_local)] * (STATS - len(stats))
    stats = everyone(jnp.stack(stats).reshape(1, STATS * count))
    coefficient, log_norm, loss_value = solve(stats, feat_all, targets_all)
    coefficient = coefficient.T
    grad_logits = -jnp.sum(coefficient, axis=1, keepdims=True) * jnp.exp(logits - log_norm.T)
    for word, mark in enumerate(marks):
        grad_logits = grad_logits + jnp.where(mark, coefficient[:, word : word + 1], 0.0)
    grad_logits = grad_logits.astype(LOW)
    grad_feat = einsum("gv,vd->gd", grad_logits, table_anchor)
    grad_feat = jnp.sum(lax.all_to_all(grad_feat, ALL, 0, 0, tiled=True), axis=0)

    grad_final = jnp.where(live[:, None], (grad_feat / length_float)[None, :], 0.0)
    grad_two, gain_two, bias_two_grad = norm_backward(
        grad_final, normed_two, inverse_two, gain_anchor[2]
    )

    grad_ffn = grad_two.astype(LOW)
    grad_down = einsum("td,the->hde", grad_ffn, activated).astype(LOW)
    grad_act = einsum("td,hde->the", grad_ffn, down_full)
    grad_pre = (slope * grad_act).astype(LOW)
    grad_up = einsum("td,the->hde", ffn_input, grad_pre).astype(LOW)
    grad_hidden = grad_two + einsum("the,hde->td", grad_pre, up_full)
    grad_one, gain_one, bias_one_grad = norm_backward(
        grad_hidden, normed_one, inverse_one, gain_anchor[1]
    )
    grad_attn = grad_one.astype(LOW)
    grad_out = einsum("td,the->hde", grad_attn, attended).astype(LOW)
    grad_att = einsum("td,hde->the", grad_attn, out_full).astype(LOW)
    grad_att = grad_att.reshape(SEQ, n_heads * local_heads, HDIM)
    grad_prob = einsum("qhd,khd->hqk", grad_att, value)
    grad_value = einsum("hqk,qhd->khd", probs_low, grad_att)
    delta_sum = jnp.sum(probs * grad_prob, axis=-1, keepdims=True)
    grad_score = (probs * (grad_prob - delta_sum)).astype(LOW)
    grad_query = einsum("hqk,khd->qhd", grad_score, key) * HDIM ** (-0.5)
    grad_key = einsum("hqk,qhd->khd", grad_score, query) * HDIM ** (-0.5)
    grad_rows = jnp.concatenate(
        [
            part.astype(LOW).reshape(SEQ, n_heads, group_wide)
            for part in (grad_query, grad_key, grad_value)
        ],
        axis=2,
    )
    grad_qkv = einsum("td,the->hde", attn_in, grad_rows).astype(LOW)
    grad_attn_all = jnp.concatenate([grad_qkv, grad_out], axis=2)
    grad_down, grad_up, grad_attn_all = owned([grad_down, grad_up, grad_attn_all])
    grad_start = grad_one + einsum("the,hde->td", grad_rows, attn_all[:, :, :three])
    grad_embed, gain_zero, bias_zero = norm_backward(
        grad_start, normed_zero, inverse_zero, gain_anchor[0]
    )
    grad_embed = grad_embed.astype(LOW)
    table_term = einsum("gv,gd->vd", grad_logits, feat_all) + give(0, wanted_first, grad_embed)
    table_grad = more(table_term, lambda turn: give(turn, asked(turn), grad_embed))

    norm_grads = jnp.stack(
        [gain_zero, gain_one, gain_two, bias_zero, bias_one_grad, bias_two_grad]
    )
    pieces = lax.all_to_all(norm_grads.reshape(count, -1), ALL, 0, 0, tiled=True)
    piece = jnp.sum(pieces, axis=0, keepdims=True)
    gain_grad, bias_grad = everyone(piece).reshape(2, 3, D)
    squares = sum(
        jnp.sum(part * part) for part in (table_grad, grad_attn_all, grad_up, grad_down, piece)
    )
    squares = jnp.sum(everyone(jnp.broadcast_to(squares, (1, 128)))[:, 0])
    clip_scale = jnp.minimum(1.0, CLIP_NORM / jnp.sqrt(squares))
    steps_done = step_count[0].astype(jnp.float32)
    bias_one = 1.0 - jnp.power(BETA_ONE, steps_done)
    bias_two = 1.0 - jnp.power(BETA_TWO, steps_done)
    rates = (clip_scale, bias_one, bias_two)

    def with_out(qkv, out):
        return jnp.concatenate([qkv, out.T[None]], axis=0)

    height = qkv_delta.shape[1]
    turned = turned_update(
        soap_owners[0] == 1,
        with_out(qkv_delta, out_delta),
        jnp.swapaxes(grad_attn_all.reshape(height, 4, group_wide), 0, 1),
        with_out(qkv_first, out_first),
        with_out(qkv_second, out_second),
        soap_basis,
        *rates,
    )
    return (
        loss_value[0, 0],
        *adam_update(table_delta, table_grad, table_first, table_second, *rates),
        *(part[:3] for part in turned),
        *(part[3].T for part in turned),
        *adam_update(up_delta, grad_up, up_first, up_second, *rates),
        *adam_update(down_delta, grad_down.T, down_first, down_second, *rates),
        *adam_update(gain_delta, gain_grad, gain_first, gain_second, *rates),
        *adam_update(bias_delta, bias_grad, bias_first, bias_second, *rates),
    )


def solution(mesh):
    group = P("rows", None)
    table = P(("heads", "rows"), None)
    qkv = P(None, "rows", "heads")
    tall = P("heads", "rows")
    wide = P("rows", "heads")
    placed = (
        group,
        P("rows"),
        group,
        group,
        P(),
        P("rows"),
        P(None, "heads", None, None),
        *(table,) * 4,
        *(qkv,) * 4,
        *(tall,) * 4,
        *(wide,) * 4,
        *(tall,) * 4,
        *(P(),) * 8,
    )
    return jax.shard_map(
        per_device,
        mesh=mesh,
        in_specs=placed,
        out_specs=(
            P(),
            *(table,) * 3,
            *(qkv,) * 3,
            *(tall,) * 3,
            *(wide,) * 3,
            *(tall,) * 3,
            *(P(),) * 6,
        ),
        check_vma=False,
    )
```

```python
import jax
import jax.numpy as jnp
from jax import lax
from jax.experimental import pallas as pl
from jax.sharding import PartitionSpec as P

D = 768
HDIM = 64
SEQ = 256
NLW = 4
CGIT = 8
STATS = 16

EPS_NORM = 1e-05
BETA_ONE = 0.9
BETA_TWO = 0.999
ADAM_EPS = 1e-08
LEARN_RATE = 0.03
DECAY_RATE = 0.01
CLIP_NORM = 1.0
CG_SHIFT = 0.002
MASKED = -1e30
HALF_ROOT = 0.7071067811865476
INV_ROOT_TAU = 0.3989422804014327
HIGH = lax.Precision.HIGHEST
ALL = ("heads", "rows")
LOW = jnp.bfloat16


def einsum(form, left, right):
    return jnp.einsum(form, left, right, preferred_element_type=jnp.float32)


def gelu_slope(values):
    return (
        0.5 * (1.0 + lax.erf(values * HALF_ROOT))
        + values * jnp.exp(-0.5 * values * values) * INV_ROOT_TAU
    )


def norm_pair(values, dots, gain, bias, gain_dot, bias_dot):
    center = values - jnp.mean(values, axis=-1, keepdims=True)
    inverse = lax.rsqrt(jnp.mean(center * center, axis=-1, keepdims=True) + EPS_NORM)
    normed = center * inverse
    normed_dot = inverse * (
        dots
        - jnp.mean(dots, axis=-1, keepdims=True)
        - normed * jnp.mean(normed * dots, axis=-1, keepdims=True)
    )
    return (normed * gain + bias, normed_dot * gain + normed * gain_dot + bias_dot, normed, inverse)


def norm_backward(grad_out, normed, inverse, gain):
    scaled = grad_out * gain
    grad_in = inverse * (
        scaled
        - jnp.mean(scaled, axis=-1, keepdims=True)
        - normed * jnp.mean(scaled * normed, axis=-1, keepdims=True)
    )
    return (grad_in, jnp.sum(grad_out * normed, axis=0), jnp.sum(grad_out, axis=0))


def everyone(block):
    count = lax.axis_size(ALL[0]) * lax.axis_size(ALL[1])
    return lax.all_to_all(
        jnp.broadcast_to(block, (count, block.shape[1])), ALL, 0, 0, tiled=True
    )


def bits_of(axis):
    return [(axis, bit) for bit in reversed(range(lax.axis_size(axis).bit_length() - 1))]


def plan():
    layout = [bit for axis in ALL for bit in bits_of(axis)]
    first = (ALL[0], 0)
    last = [bit for bit in layout if bit[0] == ALL[1] and bit[1] >= 2]
    middle = [bit for bit in layout if bit != first and bit not in last]
    return layout, first, middle, last


def swapped(block, step):
    axis, bit = step
    size = lax.axis_size(axis)
    return lax.ppermute(block, axis, [(index, index ^ (1 << bit)) for index in range(size)])


def joined(block, have, step):
    layout = plan()[0]
    axis, bit = step
    came = swapped(block, step)
    have = [other for other in layout if other in have or other == step]
    place = have.index(step)
    both = jnp.stack([block, came], axis=place)
    if axis != ALL[0]:
        upper = ((lax.axis_index(axis) >> bit) & 1) > 0
        both = jnp.where(upper, jnp.stack([came, block], axis=place), both)
    return both, have


def assembled(blocks, rows):
    layout, first, middle, last = plan()
    orders = [
        last + [middle[index] for index in turn] for turn in ((1, 0, 2), (0, 2, 1), (2, 1, 0))
    ]
    width = blocks[0].shape[1]
    states = [joined(block, [], order[0]) for block, order in zip(blocks, orders)]
    started, rows = lax.optimization_barrier(([state[0] for state in states], rows))
    results = []
    for block, (_, have), order in zip(started, states, orders):
        for step in order[1:]:
            block, have = joined(block, have, step)
        pair = (block, swapped(block, first))
        results.append([half.reshape(lax.axis_size(ALL[0]) // 2, -1, width) for half in pair])
    return results, rows


def owned(parts):
    layout, first, middle, last = plan()
    results = []
    for turn, (keep, send) in enumerate(parts):
        turn %= len(middle)
        block = (keep.astype(jnp.float32) + swapped(send, first).astype(jnp.float32)).astype(LOW)
        left = [step for step in layout if step != first]
        block = block.reshape((2,) * len(left) + (-1, keep.shape[-1]))
        for step in middle[turn:] + middle[:turn] + last[::-1]:
            axis, bit = step
            place = left.index(step)
            if axis == ALL[0]:
                keep = lax.index_in_dim(block, 0, place, keepdims=False)
                send = lax.index_in_dim(block, 1, place, keepdims=False)
            else:
                mine = (lax.axis_index(axis) >> bit) & 1
                keep = lax.dynamic_index_in_dim(block, mine, place, keepdims=False)
                send = lax.dynamic_index_in_dim(block, 1 - mine, place, keepdims=False)
            block = keep.astype(jnp.float32) + swapped(send, step).astype(jnp.float32)
            left.pop(place)
            if left:
                block = block.astype(LOW)
        results.append(block)
    return results


def solve_kernel(stats_ref, feat_ref, targets_ref, coef_ref, norm_ref, loss_ref):
    count = feat_ref.shape[0]

    def stat(index):
        return stats_ref[:, index * count : (index + 1) * count]

    peaks = stat(0)
    peak = jnp.max(peaks, axis=0, keepdims=True)
    scale = jnp.exp(peaks - peak)
    mass = jnp.sum(stat(1) * scale, axis=0, keepdims=True)
    weighted = jnp.sum(stat(2) * scale, axis=0, keepdims=True)
    log_norm = peak + jnp.log(mass)
    shift = log_norm + weighted / mass
    picked = [
        jnp.sum(stat(3 + word) + stat(3 + NLW + word), axis=0, keepdims=True)
        for word in range(NLW)
    ]
    differ = jnp.concatenate(picked, axis=0) - shift - targets_ref[...]
    feat = feat_ref[...].astype(jnp.float32)
    center = feat - jnp.mean(feat, axis=0, keepdims=True)
    kernel = (
        lax.dot_general(
            center,
            center,
            (((1,), (1,)), ((), ())),
            precision=HIGH,
            preferred_element_type=jnp.float32,
        )
        / D
    )
    answer = jnp.zeros_like(differ)
    residual = differ
    direction = differ
    norm_now = jnp.sum(residual * residual, axis=1, keepdims=True)
    for step in range(CGIT):
        image = (
            jnp.dot(direction, kernel, precision=HIGH, preferred_element_type=jnp.float32)
            + CG_SHIFT * direction
        )
        alpha = norm_now / jnp.sum(direction * image, axis=1, keepdims=True)
        answer = answer + alpha * direction
        residual = residual - alpha * image
        if step + 1 < CGIT:
            norm_next = jnp.sum(residual * residual, axis=1, keepdims=True)
            direction = residual + norm_next / norm_now * direction
            norm_now = norm_next
    coef_ref[...] = 2.0 * answer / NLW
    norm_ref[...] = log_norm
    squares = jnp.sum(differ * differ, axis=1, keepdims=True)
    loss_ref[...] = jnp.sum(squares, axis=0, keepdims=True) / NLW


def solve(stats, feat, targets):
    count = feat.shape[0]
    return pl.pallas_call(
        solve_kernel,
        out_shape=(
            jax.ShapeDtypeStruct((NLW, count), jnp.float32),
            jax.ShapeDtypeStruct((1, count), jnp.float32),
            jax.ShapeDtypeStruct((1, 1), jnp.float32),
        ),
    )(stats, feat, targets)


def adam_moments(gradient, moment_one, moment_two, bias_one, bias_two):
    new_one = BETA_ONE * moment_one + (1.0 - BETA_ONE) * gradient
    new_two = BETA_TWO * moment_two + (1.0 - BETA_TWO) * gradient * gradient
    return (new_one / bias_one / (jnp.sqrt(new_two / bias_two) + ADAM_EPS), new_one, new_two)


def adam_update(master, gradient, moment_one, moment_two, clip_scale, bias_one, bias_two):
    direction, new_one, new_two = adam_moments(
        clip_scale * gradient, moment_one, moment_two, bias_one, bias_two
    )
    return (master - LEARN_RATE * (direction + DECAY_RATE * master), new_one, new_two)


def turned_update(owner, master, gradient, first, second, basis, clip_scale, bias_one, bias_two):
    count, height, width = gradient.shape

    def grouped(array):
        return array.reshape(count, height, width // HDIM, HDIM)

    plain = clip_scale * gradient
    turned = jnp.einsum("ciha,chab->cihb", grouped(plain), basis, precision=HIGH)
    used = jnp.where(owner, turned.reshape(gradient.shape), plain)
    direction, new_one, new_two = adam_moments(used, first, second, bias_one, bias_two)
    back = jnp.einsum("cihb,chab->ciha", grouped(direction), basis, precision=HIGH)
    direction = jnp.where(owner, back.reshape(gradient.shape), direction)
    return (master - LEARN_RATE * (direction + DECAY_RATE * master), new_one, new_two)


def per_device(
    token_ids,
    lengths,
    label_ids,
    targets,
    step_count,
    soap_owners,
    soap_basis,
    table_anchor,
    table_delta,
    table_first,
    table_second,
    qkv_anchor,
    qkv_delta,
    qkv_first,
    qkv_second,
    out_anchor,
    out_delta,
    out_first,
    out_second,
    up_anchor,
    up_delta,
    up_first,
    up_second,
    down_anchor,
    down_delta,
    down_first,
    down_second,
    gain_anchor,
    gain_delta,
    gain_first,
    gain_second,
    bias_anchor,
    bias_delta,
    bias_first,
    bias_second,
):
    n_heads = lax.axis_size("heads")
    n_rows = lax.axis_size("rows")
    count = n_heads * n_rows
    head_index = lax.axis_index("heads")
    me = head_index * n_rows + lax.axis_index("rows")
    vocab = table_anchor.shape[0]
    group_wide = qkv_anchor.shape[2]
    local_heads = group_wide // HDIM

    def side_by_side(qkv, out):
        return jnp.concatenate([qkv[0], qkv[1], qkv[2], out.T], axis=1)

    def packed(anchor, delta):
        return jnp.concatenate([anchor, delta.astype(LOW)], axis=1)

    blocks = [
        packed(side_by_side(qkv_anchor, out_anchor), side_by_side(qkv_delta, out_delta)),
        packed(up_anchor, up_delta),
        packed(down_anchor.T, down_delta.T),
    ]

    room = 8 * -(-(2 * SEQ // count + 8) // 8)
    slots = count * room
    ids = lax.dynamic_index_in_dim(token_ids, head_index, 0, keepdims=False)
    owner = ids // vocab
    local = ids - owner * vocab
    place = lax.iota(jnp.int32, SEQ)
    same = ids[:, None] == ids[None, :]
    earliest = jnp.min(jnp.where(same, place[None, :], SEQ), axis=1)
    leads = earliest == place
    rank = jnp.sum(
        (leads[None, :] & (owner[:, None] == owner[None, :]) & (place[None, :] < earliest[:, None])),
        axis=1,
        dtype=jnp.int32,
    )
    longest = jnp.max(rank) + 1
    own_labels = lax.dynamic_index_in_dim(label_ids, head_index, 0, keepdims=False)
    own_targets = lax.dynamic_index_in_dim(targets, head_index, 0, keepdims=False)
    notes = jnp.concatenate(
        [longest[None].astype(jnp.float32), own_labels.astype(jnp.float32), own_targets]
    )
    both = jnp.concatenate([table_anchor, table_delta.astype(LOW)], axis=1)

    def slot_of(turn):
        within = rank - turn * room
        return jnp.where((within >= 0) & (within < room), owner * room + within, -1)

    def wanted_of(turn):
        taken = jnp.where(leads, slot_of(turn), -1)
        hit = lax.iota(jnp.int32, slots)[:, None] == taken[None, :]
        return (jnp.sum(jnp.where(hit, local[None, :] + 1, 0), axis=1) - 1).reshape(count, room)

    def asked(turn):
        return lax.all_to_all(wanted_of(turn), ALL, 0, 0, tiled=True).reshape(slots)

    def chosen(wanted):
        return (wanted[:, None] == lax.broadcasted_iota(jnp.int32, (slots, vocab), 1)).astype(LOW)

    def token_slots(turn):
        return (
            slot_of(turn)[:, None] == lax.broadcasted_iota(jnp.int32, (SEQ, slots), 1)
        ).astype(LOW)

    def rows_of(wanted):
        return einsum("sv,vd->sd", chosen(wanted), both).astype(LOW)

    def fetch(turn, rows):
        rows = lax.all_to_all(rows.reshape(count, room, 2 * D), ALL, 0, 0, tiled=True)
        return einsum("ts,sd->td", token_slots(turn), rows.reshape(slots, 2 * D))

    def give(turn, wanted, grads):
        sums = einsum("ts,td->sd", token_slots(turn), grads).astype(LOW)
        sums = lax.all_to_all(sums.reshape(count, room, D), ALL, 0, 0, tiled=True)
        return einsum("sv,sd->vd", chosen(wanted), sums.reshape(slots, D))

    def more(start, step):
        def rest(value):
            return lax.fori_loop(1, rounds, lambda turn, so_far: so_far + step(turn), value)

        return lax.cond(rounds > 1, rest, lambda value: value, start)

    message = jnp.concatenate(
        [
            wanted_of(0).astype(jnp.float32),
            jnp.broadcast_to(notes[None], (count, notes.shape[0])),
        ],
        axis=1,
    )
    message = lax.all_to_all(message, ALL, 0, 0, tiled=True)
    wanted_first = message[:, :room].astype(jnp.int32).reshape(slots)
    rounds = -(-jnp.max(message[:, room]).astype(jnp.int32) // room)
    labels = message[:, room + 1 : room + 1 + NLW].astype(jnp.int32) - me * vocab
    targets_all = message[:, room + 1 + NLW :].T
    (attn_pair, up_pair, down_pair), rows_first = assembled(blocks, rows_of(wanted_first))
    embedded_both = more(fetch(0, rows_first), lambda turn: fetch(turn, rows_of(asked(turn))))
    start_x, start_dot, normed_zero, inverse_zero = norm_pair(
        embedded_both[:, :D],
        embedded_both[:, D:],
        gain_anchor[0],
        bias_anchor[0],
        gain_delta[0],
        bias_delta[0],
    )

    own_length = lax.dynamic_index_in_dim(lengths, head_index, 0, keepdims=False)
    live = lax.iota(jnp.int32, SEQ) < own_length
    length_float = own_length.astype(jnp.float32)

    attn_in = start_x.astype(LOW)
    attn_dot_in = start_dot.astype(LOW)
    three = 3 * group_wide
    wide = attn_pair[0].shape[2] // 2
    groups = attn_pair[0].shape[0]
    qkv_full = [half[:, :, :three] for half in attn_pair]
    out_full = [half[:, :, three:wide] for half in attn_pair]
    out_step = [half[:, :, wide + three :] for half in attn_pair]

    def into(values, pair):
        return [einsum("td,hde->the", values, half) for half in pair]

    def out_of(values, pair):
        return sum(einsum("the,hde->td", part, half) for part, half in zip(values, pair))

    def halves(values):
        return [values[:, :groups], values[:, groups:]]

    through = into(attn_in, attn_pair)
    projected = jnp.concatenate([part[:, :, :three].astype(LOW) for part in through], axis=1)
    projected_dot = jnp.concatenate(
        [
            (part[:, :, wide : wide + three] + more_part).astype(LOW)
            for part, more_part in zip(through, into(attn_dot_in, qkv_full))
        ],
        axis=1,
    )

    def split_heads(array):
        array = array.reshape(SEQ, n_heads, 3, local_heads, HDIM)
        return [array[:, :, index].reshape(SEQ, n_heads * local_heads, HDIM) for index in range(3)]

    query, key, value = split_heads(projected)
    query_dot, key_dot, value_dot = split_heads(projected_dot)
    scores = einsum("qhd,khd->hqk", query, key) * HDIM ** (-0.5)
    scores = jnp.where(live[None, None, :], scores, MASKED)
    exponent = jnp.exp(scores - jnp.max(scores, axis=-1, keepdims=True))
    probs = exponent / jnp.sum(exponent, axis=-1, keepdims=True)
    probs_low = probs.astype(LOW)
    score_dot = (
        einsum("qhd,khd->hqk", query_dot, key) + einsum("qhd,khd->hqk", query, key_dot)
    ) * HDIM ** (-0.5)
    prob_dot = (probs * (score_dot - jnp.sum(probs * score_dot, axis=-1, keepdims=True))).astype(LOW)
    attended = einsum("hqk,khd->qhd", probs_low, value).astype(LOW)
    attended_dot = (
        einsum("hqk,khd->qhd", prob_dot, value) + einsum("hqk,khd->qhd", probs_low, value_dot)
    ).astype(LOW)
    attended = halves(attended.reshape(SEQ, n_heads, group_wide))
    attended_dot = halves(attended_dot.reshape(SEQ, n_heads, group_wide))
    attn_out = out_of(attended, out_full)
    attn_dot = out_of(attended_dot, out_full) + out_of(attended, out_step)
    hidden, hidden_dot, normed_one, inverse_one = norm_pair(
        start_x + attn_out,
        start_dot + attn_dot,
        gain_anchor[1],
        bias_anchor[1],
        gain_delta[1],
        bias_delta[1],
    )
    ffn_input = hidden.astype(LOW)
    up_full, up_step = zip(*(jnp.split(half, 2, axis=2) for half in up_pair))
    down_full, down_step = zip(*(jnp.split(half, 2, axis=2) for half in down_pair))
    pre_gelu = into(ffn_input, up_full)
    pre_dot = [
        part + more_part
        for part, more_part in zip(into(hidden_dot.astype(LOW), up_full), into(ffn_input, up_step))
    ]
    activated = [jax.nn.gelu(part, approximate=False).astype(LOW) for part in pre_gelu]
    slope = [gelu_slope(part) for part in pre_gelu]
    act_dot = [(part * dot).astype(LOW) for part, dot in zip(slope, pre_dot)]
    ffn_out = out_of(activated, down_full)
    ffn_dot = out_of(act_dot, down_full) + out_of(activated, down_step)
    final_out, final_dot, normed_two, inverse_two = norm_pair(
        hidden + ffn_out,
        hidden_dot + ffn_dot,
        gain_anchor[2],
        bias_anchor[2],
        gain_delta[2],
        bias_delta[2],
    )

    def pooled(values):
        return (jnp.sum(jnp.where(live[:, None], values, 0.0), axis=0) / length_float).astype(LOW)

    feats = everyone(jnp.concatenate([pooled(final_dot), pooled(final_out)])[None])
    feat_all = feats[:, D:]
    logits = einsum("gd,vd->gv", feat_all, table_anchor)
    logit_dot = einsum("gd,vd->gv", feats, both)
    vocab_iota = lax.broadcasted_iota(jnp.int32, logits.shape, 1)
    marks = [vocab_iota == labels[:, word : word + 1] for word in range(NLW)]
    peak_local = jnp.max(logits, axis=1)
    exponent = jnp.exp(logits - peak_local[:, None])
    stats = [peak_local, jnp.sum(exponent, axis=1), jnp.sum(exponent * logit_dot, axis=1)]
    stats += [jnp.sum(jnp.where(mark, logits, 0.0), axis=1) for mark in marks]
    stats += [jnp.sum(jnp.where(mark, logit_dot, 0.0), axis=1) for mark in marks]
    stats += [jnp.zeros_like(peak_local)] * (STATS - len(stats))
    stats = everyone(jnp.stack(stats).reshape(1, STATS * count))
    coefficient, log_norm, loss_value = solve(stats, feat_all, targets_all)
    coefficient = coefficient.T
    grad_logits = -jnp.sum(coefficient, axis=1, keepdims=True) * jnp.exp(logits - log_norm.T)
    for word, mark in enumerate(marks):
        grad_logits = grad_logits + jnp.where(mark, coefficient[:, word : word + 1], 0.0)
    grad_logits = grad_logits.astype(LOW)
    grad_feat = einsum("gv,vd->gd", grad_logits, table_anchor)
    grad_feat = jnp.sum(lax.all_to_all(grad_feat, ALL, 0, 0, tiled=True), axis=0)

    grad_final = jnp.where(live[:, None], (grad_feat / length_float)[None, :], 0.0)
    grad_two, gain_two, bias_two_grad = norm_backward(
        grad_final, normed_two, inverse_two, gain_anchor[2]
    )

    grad_ffn = grad_two.astype(LOW)

    def outer(left, pair):
        return [einsum("td,the->hde", left, part).astype(LOW) for part in pair]

    grad_down = outer(grad_ffn, activated)
    grad_act = into(grad_ffn, down_full)
    grad_pre = [(part * grad).astype(LOW) for part, grad in zip(slope, grad_act)]
    grad_up = outer(ffn_input, grad_pre)
    grad_hidden = grad_two + out_of(grad_pre, up_full)
    grad_one, gain_one, bias_one_grad = norm_backward(
        grad_hidden, normed_one, inverse_one, gain_anchor[1]
    )
    grad_attn = grad_one.astype(LOW)
    grad_att = jnp.concatenate([part.astype(LOW) for part in into(grad_attn, out_full)], axis=1)
    grad_att = grad_att.reshape(SEQ, n_heads * local_heads, HDIM)
    grad_prob = einsum("qhd,khd->hqk", grad_att, value)
    grad_value = einsum("hqk,qhd->khd", probs_low, grad_att)
    delta_sum = jnp.sum(probs * grad_prob, axis=-1, keepdims=True)
    grad_score = (probs * (grad_prob - delta_sum)).astype(LOW)
    grad_query = einsum("hqk,khd->qhd", grad_score, key) * HDIM ** (-0.5)
    grad_key = einsum("hqk,qhd->khd", grad_score, query) * HDIM ** (-0.5)
    grad_rows = jnp.concatenate(
        [
            part.astype(LOW).reshape(SEQ, n_heads, group_wide)
            for part in (grad_query, grad_key, grad_value)
        ],
        axis=2,
    )
    grad_rows = halves(grad_rows)
    stacked = [
        jnp.concatenate(
            [
                jnp.pad(rows, ((0, 0), (0, 0), (0, wide - three))),
                jnp.pad(part, ((0, 0), (0, 0), (three, 0))),
            ],
            axis=0,
        )
        for rows, part in zip(grad_rows, attended)
    ]
    grad_attn_all = outer(jnp.concatenate([attn_in, grad_attn], axis=0), stacked)
    grad_down, grad_up, grad_attn_all = owned([grad_down, grad_up, grad_attn_all])
    grad_start = grad_one + out_of(grad_rows, qkv_full)
    grad_embed, gain_zero, bias_zero = norm_backward(
        grad_start, normed_zero, inverse_zero, gain_anchor[0]
    )
    grad_embed = grad_embed.astype(LOW)
    table_term = einsum("gv,gd->vd", grad_logits, feat_all) + give(0, wanted_first, grad_embed)
    table_grad = more(table_term, lambda turn: give(turn, asked(turn), grad_embed))

    norm_grads = jnp.stack(
        [gain_zero, gain_one, gain_two, bias_zero, bias_one_grad, bias_two_grad]
    )
    pieces = lax.all_to_all(norm_grads.reshape(count, -1), ALL, 0, 0, tiled=True)
    piece = jnp.sum(pieces, axis=0, keepdims=True)
    gain_grad, bias_grad = everyone(piece).reshape(2, 3, D)
    squares = sum(
        jnp.sum(part * part) for part in (table_grad, grad_attn_all, grad_up, grad_down, piece)
    )
    squares = jnp.sum(everyone(jnp.broadcast_to(squares, (1, 128)))[:, 0])
    clip_scale = jnp.minimum(1.0, CLIP_NORM / jnp.sqrt(squares))
    steps_done = step_count[0].astype(jnp.float32)
    bias_one = 1.0 - jnp.power(BETA_ONE, steps_done)
    bias_two = 1.0 - jnp.power(BETA_TWO, steps_done)
    rates = (clip_scale, bias_one, bias_two)

    def with_out(qkv, out):
        return jnp.concatenate([qkv, out.T[None]], axis=0)

    height = qkv_delta.shape[1]
    turned = turned_update(
        soap_owners[0] == 1,
        with_out(qkv_delta, out_delta),
        jnp.swapaxes(grad_attn_all.reshape(height, 4, group_wide), 0, 1),
        with_out(qkv_first, out_first),
        with_out(qkv_second, out_second),
        soap_basis,
        *rates,
    )
    return (
        loss_value[0, 0],
        *adam_update(table_delta, table_grad, table_first, table_second, *rates),
        *(part[:3] for part in turned),
        *(part[3].T for part in turned),
        *adam_update(up_delta, grad_up, up_first, up_second, *rates),
        *adam_update(down_delta, grad_down.T, down_first, down_second, *rates),
        *adam_update(gain_delta, gain_grad, gain_first, gain_second, *rates),
        *adam_update(bias_delta, bias_grad, bias_first, bias_second, *rates),
    )


def solution(mesh):
    group = P("rows", None)
    table = P(("heads", "rows"), None)
    qkv = P(None, "rows", "heads")
    tall = P("heads", "rows")
    wide = P("rows", "heads")
    placed = (
        group,
        P("rows"),
        group,
        group,
        P(),
        P("rows"),
        P(None, "heads", None, None),
        *(table,) * 4,
        *(qkv,) * 4,
        *(tall,) * 4,
        *(wide,) * 4,
        *(tall,) * 4,
        *(P(),) * 8,
    )
    return jax.shard_map(
        per_device,
        mesh=mesh,
        in_specs=placed,
        out_specs=(
            P(),
            *(table,) * 3,
            *(qkv,) * 3,
            *(tall,) * 3,
            *(wide,) * 3,
            *(tall,) * 3,
            *(P(),) * 6,
        ),
        check_vma=False,
    )
```

```python
import jax
import jax.numpy as jnp
from jax import lax
from jax.experimental import pallas as pl
from jax.sharding import PartitionSpec as P

D = 768
HDIM = 64
SEQ = 256
NLW = 4
CGIT = 8
STATS = 16

EPS_NORM = 1e-05
BETA_ONE = 0.9
BETA_TWO = 0.999
ADAM_EPS = 1e-08
LEARN_RATE = 0.03
DECAY_RATE = 0.01
CLIP_NORM = 1.0
CG_SHIFT = 0.002
MASKED = -1e30
HALF_ROOT = 0.7071067811865476
INV_ROOT_TAU = 0.3989422804014327
HIGH = lax.Precision.HIGHEST
ALL = ("heads", "rows")
LOW = jnp.bfloat16


def einsum(form, left, right):
    return jnp.einsum(form, left, right, preferred_element_type=jnp.float32)


def gelu_slope(values):
    return (
        0.5 * (1.0 + lax.erf(values * HALF_ROOT))
        + values * jnp.exp(-0.5 * values * values) * INV_ROOT_TAU
    )


def norm_pair(values, dots, gain, bias, gain_dot, bias_dot):
    center = values - jnp.mean(values, axis=-1, keepdims=True)
    inverse = lax.rsqrt(jnp.mean(center * center, axis=-1, keepdims=True) + EPS_NORM)
    normed = center * inverse
    normed_dot = inverse * (
        dots
        - jnp.mean(dots, axis=-1, keepdims=True)
        - normed * jnp.mean(normed * dots, axis=-1, keepdims=True)
    )
    return (normed * gain + bias, normed_dot * gain + normed * gain_dot + bias_dot, normed, inverse)


def norm_backward(grad_out, normed, inverse, gain):
    scaled = grad_out * gain
    grad_in = inverse * (
        scaled
        - jnp.mean(scaled, axis=-1, keepdims=True)
        - normed * jnp.mean(scaled * normed, axis=-1, keepdims=True)
    )
    return (grad_in, jnp.sum(grad_out * normed, axis=0), jnp.sum(grad_out, axis=0))


def everyone(block):
    count = lax.axis_size(ALL[0]) * lax.axis_size(ALL[1])
    return lax.all_to_all(
        jnp.broadcast_to(block, (count, block.shape[1])), ALL, 0, 0, tiled=True
    )


def bits_of(axis):
    return [(axis, bit) for bit in reversed(range(lax.axis_size(axis).bit_length() - 1))]


def plan():
    layout = [bit for axis in ALL for bit in bits_of(axis)]
    first = (ALL[0], 0)
    last = [bit for bit in layout if bit[0] == ALL[1] and bit[1] >= 2]
    middle = [bit for bit in layout if bit != first and bit not in last]
    return layout, first, middle, last


def halved(block, left, step):
    axis, bit = step
    place = left.index(step)
    mine = (lax.axis_index(axis) >> bit) & 1
    send = lax.dynamic_index_in_dim(block, 1 - mine, place, keepdims=False)
    keep = lax.dynamic_index_in_dim(block, mine, place, keepdims=False)
    size = lax.axis_size(axis)
    came = lax.ppermute(send, axis, [(index, index ^ (1 << bit)) for index in range(size)])
    block = keep.astype(jnp.float32) + came.astype(jnp.float32)
    left = [other for other in left if other != step]
    return (block.astype(LOW) if left else block), left


def begun(part):
    layout, first, _, _ = plan()
    block = part.reshape((2,) * len(layout) + (-1, part.shape[-1]))
    return halved(block, layout, first)[0]


def finished(blocks, turns):
    layout, first, middle, last = plan()
    results = []
    for block, turn in zip(blocks, turns):
        left = [bit for bit in layout if bit != first]
        for step in middle[turn:] + middle[:turn] + last[::-1]:
            block, left = halved(block, left, step)
        results.append(block)
    return results


def solve_kernel(stats_ref, feat_ref, targets_ref, coef_ref, norm_ref, loss_ref):
    count = feat_ref.shape[0]

    def stat(index):
        return stats_ref[:, index * count : (index + 1) * count]

    peaks = stat(0)
    peak = jnp.max(peaks, axis=0, keepdims=True)
    scale = jnp.exp(peaks - peak)
    mass = jnp.sum(stat(1) * scale, axis=0, keepdims=True)
    weighted = jnp.sum(stat(2) * scale, axis=0, keepdims=True)
    log_norm = peak + jnp.log(mass)
    shift = log_norm + weighted / mass
    picked = [
        jnp.sum(stat(3 + word) + stat(3 + NLW + word), axis=0, keepdims=True)
        for word in range(NLW)
    ]
    differ = jnp.concatenate(picked, axis=0) - shift - targets_ref[...]
    feat = feat_ref[...].astype(jnp.float32)
    center = feat - jnp.mean(feat, axis=0, keepdims=True)
    kernel = (
        lax.dot_general(
            center,
            center,
            (((1,), (1,)), ((), ())),
            precision=HIGH,
            preferred_element_type=jnp.float32,
        )
        / D
    )
    answer = jnp.zeros_like(differ)
    residual = differ
    direction = differ
    norm_now = jnp.sum(residual * residual, axis=1, keepdims=True)
    for step in range(CGIT):
        image = (
            jnp.dot(direction, kernel, precision=HIGH, preferred_element_type=jnp.float32)
            + CG_SHIFT * direction
        )
        alpha = norm_now / jnp.sum(direction * image, axis=1, keepdims=True)
        answer = answer + alpha * direction
        residual = residual - alpha * image
        if step + 1 < CGIT:
            norm_next = jnp.sum(residual * residual, axis=1, keepdims=True)
            direction = residual + norm_next / norm_now * direction
            norm_now = norm_next
    coef_ref[...] = 2.0 * answer / NLW
    norm_ref[...] = log_norm
    squares = jnp.sum(differ * differ, axis=1, keepdims=True)
    loss_ref[...] = jnp.sum(squares, axis=0, keepdims=True) / NLW


def solve(stats, feat, targets):
    count = feat.shape[0]
    return pl.pallas_call(
        solve_kernel,
        out_shape=(
            jax.ShapeDtypeStruct((NLW, count), jnp.float32),
            jax.ShapeDtypeStruct((1, count), jnp.float32),
            jax.ShapeDtypeStruct((1, 1), jnp.float32),
        ),
    )(stats, feat, targets)


def adam_moments(gradient, moment_one, moment_two, bias_one, bias_two):
    new_one = BETA_ONE * moment_one + (1.0 - BETA_ONE) * gradient
    new_two = BETA_TWO * moment_two + (1.0 - BETA_TWO) * gradient * gradient
    return (new_one / bias_one / (jnp.sqrt(new_two / bias_two) + ADAM_EPS), new_one, new_two)


def adam_update(master, gradient, moment_one, moment_two, clip_scale, bias_one, bias_two):
    direction, new_one, new_two = adam_moments(
        clip_scale * gradient, moment_one, moment_two, bias_one, bias_two
    )
    return (master - LEARN_RATE * (direction + DECAY_RATE * master), new_one, new_two)


def turned_update(owner, master, gradient, first, second, basis, clip_scale, bias_one, bias_two):
    count, height, width = gradient.shape

    def grouped(array):
        return array.reshape(count, height, width // HDIM, HDIM)

    plain = clip_scale * gradient
    turned = jnp.einsum("ciha,chab->cihb", grouped(plain), basis, precision=HIGH)
    used = jnp.where(owner, turned.reshape(gradient.shape), plain)
    direction, new_one, new_two = adam_moments(used, first, second, bias_one, bias_two)
    back = jnp.einsum("cihb,chab->ciha", grouped(direction), basis, precision=HIGH)
    direction = jnp.where(owner, back.reshape(gradient.shape), direction)
    return (master - LEARN_RATE * (direction + DECAY_RATE * master), new_one, new_two)


def per_device(
    token_ids,
    lengths,
    label_ids,
    targets,
    step_count,
    soap_owners,
    soap_basis,
    table_anchor,
    table_delta,
    table_first,
    table_second,
    qkv_anchor,
    qkv_delta,
    qkv_first,
    qkv_second,
    out_anchor,
    out_delta,
    out_first,
    out_second,
    up_anchor,
    up_delta,
    up_first,
    up_second,
    down_anchor,
    down_delta,
    down_first,
    down_second,
    gain_anchor,
    gain_delta,
    gain_first,
    gain_second,
    bias_anchor,
    bias_delta,
    bias_first,
    bias_second,
):
    n_heads = lax.axis_size("heads")
    n_rows = lax.axis_size("rows")
    count = n_heads * n_rows
    head_index = lax.axis_index("heads")
    me = head_index * n_rows + lax.axis_index("rows")
    vocab = table_anchor.shape[0]
    group_wide = qkv_anchor.shape[2]
    local_heads = group_wide // HDIM

    def side_by_side(qkv, out):
        return jnp.concatenate([qkv[0], qkv[1], qkv[2], out.T], axis=1)

    def gathered(anchor, delta):
        block = jnp.concatenate([anchor, delta.astype(LOW)], axis=1)
        full = lax.all_gather(block, ALL, axis=0, tiled=True)
        return full.reshape(n_heads, D, block.shape[1])

    attn_all = gathered(side_by_side(qkv_anchor, out_anchor), side_by_side(qkv_delta, out_delta))
    ffn_all = gathered(
        jnp.concatenate([up_anchor, down_anchor.T], axis=1),
        jnp.concatenate([up_delta, down_delta.T], axis=1),
    )

    room = 8 * -(-(2 * SEQ // count + 8) // 8)
    slots = count * room
    ids = lax.dynamic_index_in_dim(token_ids, head_index, 0, keepdims=False)
    owner = ids // vocab
    local = ids - owner * vocab
    place = lax.iota(jnp.int32, SEQ)
    same = ids[:, None] == ids[None, :]
    earliest = jnp.min(jnp.where(same, place[None, :], SEQ), axis=1)
    leads = earliest == place
    rank = jnp.sum(
        (leads[None, :] & (owner[:, None] == owner[None, :]) & (place[None, :] < earliest[:, None])),
        axis=1,
        dtype=jnp.int32,
    )
    longest = jnp.max(rank) + 1
    own_labels = lax.dynamic_index_in_dim(label_ids, head_index, 0, keepdims=False)
    own_targets = lax.dynamic_index_in_dim(targets, head_index, 0, keepdims=False)
    notes = jnp.concatenate(
        [longest[None].astype(jnp.float32), own_labels.astype(jnp.float32), own_targets]
    )
    both = jnp.concatenate([table_anchor, table_delta.astype(LOW)], axis=1)

    def slot_of(turn):
        within = rank - turn * room
        return jnp.where((within >= 0) & (within < room), owner * room + within, -1)

    def wanted_of(turn):
        taken = jnp.where(leads, slot_of(turn), -1)
        hit = lax.iota(jnp.int32, slots)[:, None] == taken[None, :]
        return (jnp.sum(jnp.where(hit, local[None, :] + 1, 0), axis=1) - 1).reshape(count, room)

    def asked(turn):
        return lax.all_to_all(wanted_of(turn), ALL, 0, 0, tiled=True).reshape(slots)

    def chosen(wanted):
        return (wanted[:, None] == lax.broadcasted_iota(jnp.int32, (slots, vocab), 1)).astype(LOW)

    def token_slots(turn):
        return (
            slot_of(turn)[:, None] == lax.broadcasted_iota(jnp.int32, (SEQ, slots), 1)
        ).astype(LOW)

    def fetch(turn, wanted):
        rows = einsum("sv,vd->sd", chosen(wanted), both).astype(LOW)
        rows = lax.all_to_all(rows.reshape(count, room, 2 * D), ALL, 0, 0, tiled=True)
        return einsum("ts,sd->td", token_slots(turn), rows.reshape(slots, 2 * D))

    def give(turn, wanted, grads):
        sums = einsum("ts,td->sd", token_slots(turn), grads).astype(LOW)
        sums = lax.all_to_all(sums.reshape(count, room, D), ALL, 0, 0, tiled=True)
        return einsum("sv,sd->vd", chosen(wanted), sums.reshape(slots, D))

    def more(start, step):
        def rest(value):
            return lax.fori_loop(1, rounds, lambda turn, so_far: so_far + step(turn), value)

        return lax.cond(rounds > 1, rest, lambda value: value, start)

    message = jnp.concatenate(
        [
            wanted_of(0).astype(jnp.float32),
            jnp.broadcast_to(notes[None], (count, notes.shape[0])),
        ],
        axis=1,
    )
    message = lax.all_to_all(message, ALL, 0, 0, tiled=True)
    wanted_first = message[:, :room].astype(jnp.int32).reshape(slots)
    rounds = -(-jnp.max(message[:, room]).astype(jnp.int32) // room)
    labels = message[:, room + 1 : room + 1 + NLW].astype(jnp.int32) - me * vocab
    targets_all = message[:, room + 1 + NLW :].T
    embedded_both = more(fetch(0, wanted_first), lambda turn: fetch(turn, asked(turn)))
    start_x, start_dot, normed_zero, inverse_zero = norm_pair(
        embedded_both[:, :D],
        embedded_both[:, D:],
        gain_anchor[0],
        bias_anchor[0],
        gain_delta[0],
        bias_delta[0],
    )

    own_length = lax.dynamic_index_in_dim(lengths, head_index, 0, keepdims=False)
    live = lax.iota(jnp.int32, SEQ) < own_length
    length_float = own_length.astype(jnp.float32)

    attn_in = start_x.astype(LOW)
    attn_dot_in = start_dot.astype(LOW)
    three = 3 * group_wide
    wide = attn_all.shape[2] // 2
    through = einsum("td,hde->the", attn_in, attn_all)
    projected = through[:, :, :three].astype(LOW)
    projected_dot = (
        through[:, :, wide : wide + three]
        + einsum("td,hde->the", attn_dot_in, attn_all[:, :, :three])
    ).astype(LOW)

    def split_heads(array):
        array = array.reshape(SEQ, n_heads, 3, local_heads, HDIM)
        return [array[:, :, index].reshape(SEQ, n_heads * local_heads, HDIM) for index in range(3)]

    query, key, value = split_heads(projected)
    query_dot, key_dot, value_dot = split_heads(projected_dot)
    scores = einsum("qhd,khd->hqk", query, key) * HDIM ** (-0.5)
    scores = jnp.where(live[None, None, :], scores, MASKED)
    exponent = jnp.exp(scores - jnp.max(scores, axis=-1, keepdims=True))
    probs = exponent / jnp.sum(exponent, axis=-1, keepdims=True)
    probs_low = probs.astype(LOW)
    score_dot = (
        einsum("qhd,khd->hqk", query_dot, key) + einsum("qhd,khd->hqk", query, key_dot)
    ) * HDIM ** (-0.5)
    prob_dot = (probs * (score_dot - jnp.sum(probs * score_dot, axis=-1, keepdims=True))).astype(LOW)
    attended = einsum("hqk,khd->qhd", probs_low, value).astype(LOW)
    attended_dot = (
        einsum("hqk,khd->qhd", prob_dot, value) + einsum("hqk,khd->qhd", probs_low, value_dot)
    ).astype(LOW)
    attended = attended.reshape(SEQ, n_heads, group_wide)
    attended_dot = attended_dot.reshape(SEQ, n_heads, group_wide)
    out_full = attn_all[:, :, three:wide]
    out_step = attn_all[:, :, wide + three :]
    attn_out = einsum("the,hde->td", attended, out_full)
    attn_dot = einsum("the,hde->td", attended_dot, out_full) + einsum(
        "the,hde->td", attended, out_step
    )
    hidden, hidden_dot, normed_one, inverse_one = norm_pair(
        start_x + attn_out,
        start_dot + attn_dot,
        gain_anchor[1],
        bias_anchor[1],
        gain_delta[1],
        bias_delta[1],
    )
    ffn_input = hidden.astype(LOW)
    up_full, down_full, up_step, down_step = jnp.split(ffn_all, 4, axis=2)
    pre_gelu = einsum("td,hde->the", ffn_input, up_full)
    pre_dot = einsum("td,hde->the", hidden_dot.astype(LOW), up_full) + einsum(
        "td,hde->the", ffn_input, up_step
    )
    activated = jax.nn.gelu(pre_gelu, approximate=False).astype(LOW)
    slope = gelu_slope(pre_gelu)
    act_dot = (slope * pre_dot).astype(LOW)
    ffn_out = einsum("the,hde->td", activated, down_full)
    ffn_dot = einsum("the,hde->td", act_dot, down_full) + einsum(
        "the,hde->td", activated, down_step
    )
    final_out, final_dot, normed_two, inverse_two = norm_pair(
        hidden + ffn_out,
        hidden_dot + ffn_dot,
        gain_anchor[2],
        bias_anchor[2],
        gain_delta[2],
        bias_delta[2],
    )

    def pooled(values):
        return (jnp.sum(jnp.where(live[:, None], values, 0.0), axis=0) / length_float).astype(LOW)

    feats = everyone(jnp.concatenate([pooled(final_dot), pooled(final_out)])[None])
    feat_all = feats[:, D:]
    logits = einsum("gd,vd->gv", feat_all, table_anchor)
    logit_dot = einsum("gd,vd->gv", feats, both)
    vocab_iota = lax.broadcasted_iota(jnp.int32, logits.shape, 1)
    marks = [vocab_iota == labels[:, word : word + 1] for word in range(NLW)]
    peak_local = jnp.max(logits, axis=1)
    exponent = jnp.exp(logits - peak_local[:, None])
    stats = [peak_local, jnp.sum(exponent, axis=1), jnp.sum(exponent * logit_dot, axis=1)]
    stats += [jnp.sum(jnp.where(mark, logits, 0.0), axis=1) for mark in marks]
    stats += [jnp.sum(jnp.where(mark, logit_dot, 0.0), axis=1) for mark in marks]
    stats += [jnp.zeros_like(peak_local)] * (STATS - len(stats))
    stats = everyone(jnp.stack(stats).reshape(1, STATS * count))
    coefficient, log_norm, loss_value = solve(stats, feat_all, targets_all)
    coefficient = coefficient.T
    grad_logits = -jnp.sum(coefficient, axis=1, keepdims=True) * jnp.exp(logits - log_norm.T)
    for word, mark in enumerate(marks):
        grad_logits = grad_logits + jnp.where(mark, coefficient[:, word : word + 1], 0.0)
    grad_logits = grad_logits.astype(LOW)
    grad_feat = einsum("gv,vd->gd", grad_logits, table_anchor)
    grad_feat = jnp.sum(lax.all_to_all(grad_feat, ALL, 0, 0, tiled=True), axis=0)

    grad_final = jnp.where(live[:, None], (grad_feat / length_float)[None, :], 0.0)
    grad_two, gain_two, bias_two_grad = norm_backward(
        grad_final, normed_two, inverse_two, gain_anchor[2]
    )

    grad_ffn = grad_two.astype(LOW)
    grad_down = einsum("td,the->hde", grad_ffn, activated).astype(LOW)
    grad_act = einsum("td,hde->the", grad_ffn, down_full)
    grad_pre = (slope * grad_act).astype(LOW)
    grad_up = einsum("td,the->hde", ffn_input, grad_pre).astype(LOW)
    grad_hidden = grad_two + einsum("the,hde->td", grad_pre, up_full)
    grad_one, gain_one, bias_one_grad = norm_backward(
        grad_hidden, normed_one, inverse_one, gain_anchor[1]
    )
    grad_attn = grad_one.astype(LOW)
    begun_ffn = [begun(grad_down), begun(grad_up)]
    grad_att = einsum("td,hde->the", grad_attn, out_full).astype(LOW)
    grad_att, begun_ffn = lax.optimization_barrier((grad_att, begun_ffn))
    grad_att = grad_att.reshape(SEQ, n_heads * local_heads, HDIM)
    grad_prob = einsum("qhd,khd->hqk", grad_att, value)
    grad_value = einsum("hqk,qhd->khd", probs_low, grad_att)
    delta_sum = jnp.sum(probs * grad_prob, axis=-1, keepdims=True)
    grad_score = (probs * (grad_prob - delta_sum)).astype(LOW)
    grad_query = einsum("hqk,khd->qhd", grad_score, key) * HDIM ** (-0.5)
    grad_key = einsum("hqk,qhd->khd", grad_score, query) * HDIM ** (-0.5)
    grad_rows = jnp.concatenate(
        [
            part.astype(LOW).reshape(SEQ, n_heads, group_wide)
            for part in (grad_query, grad_key, grad_value)
        ],
        axis=2,
    )
    pair = 2 * group_wide
    grad_front = einsum("td,the->hde", attn_in, grad_rows[:, :, :pair]).astype(LOW)
    tail = jnp.concatenate(
        [
            jnp.pad(grad_rows[:, :, pair:], ((0, 0), (0, 0), (0, group_wide))),
            jnp.pad(attended, ((0, 0), (0, 0), (group_wide, 0))),
        ],
        axis=0,
    )
    grad_tail = einsum("td,the->hde", jnp.concatenate([attn_in, grad_attn], axis=0), tail)
    begun_attn = [begun(grad_front), begun(grad_tail.astype(LOW))]
    grad_down, grad_up, grad_front, grad_tail = finished(begun_ffn + begun_attn, (0, 1, 2, 0))
    grad_attn_all = jnp.concatenate([grad_front, grad_tail], axis=1)
    grad_start = grad_one + einsum("the,hde->td", grad_rows, attn_all[:, :, :three])
    grad_embed, gain_zero, bias_zero = norm_backward(
        grad_start, normed_zero, inverse_zero, gain_anchor[0]
    )
    grad_embed = grad_embed.astype(LOW)
    table_term = einsum("gv,gd->vd", grad_logits, feat_all) + give(0, wanted_first, grad_embed)
    table_grad = more(table_term, lambda turn: give(turn, asked(turn), grad_embed))

    norm_grads = jnp.stack(
        [gain_zero, gain_one, gain_two, bias_zero, bias_one_grad, bias_two_grad]
    )
    pieces = lax.all_to_all(norm_grads.reshape(count, -1), ALL, 0, 0, tiled=True)
    piece = jnp.sum(pieces, axis=0, keepdims=True)
    gain_grad, bias_grad = everyone(piece).reshape(2, 3, D)
    squares = sum(
        jnp.sum(part * part) for part in (table_grad, grad_attn_all, grad_up, grad_down, piece)
    )
    squares = jnp.sum(everyone(jnp.broadcast_to(squares, (1, 128)))[:, 0])
    clip_scale = jnp.minimum(1.0, CLIP_NORM / jnp.sqrt(squares))
    steps_done = step_count[0].astype(jnp.float32)
    bias_one = 1.0 - jnp.power(BETA_ONE, steps_done)
    bias_two = 1.0 - jnp.power(BETA_TWO, steps_done)
    rates = (clip_scale, bias_one, bias_two)

    def with_out(qkv, out):
        return jnp.concatenate([qkv, out.T[None]], axis=0)

    height = qkv_delta.shape[1]
    turned = turned_update(
        soap_owners[0] == 1,
        with_out(qkv_delta, out_delta),
        jnp.swapaxes(grad_attn_all.reshape(height, 4, group_wide), 0, 1),
        with_out(qkv_first, out_first),
        with_out(qkv_second, out_second),
        soap_basis,
        *rates,
    )
    return (
        loss_value[0, 0],
        *adam_update(table_delta, table_grad, table_first, table_second, *rates),
        *(part[:3] for part in turned),
        *(part[3].T for part in turned),
        *adam_update(up_delta, grad_up, up_first, up_second, *rates),
        *adam_update(down_delta, grad_down.T, down_first, down_second, *rates),
        *adam_update(gain_delta, gain_grad, gain_first, gain_second, *rates),
        *adam_update(bias_delta, bias_grad, bias_first, bias_second, *rates),
    )


def solution(mesh):
    group = P("rows", None)
    table = P(("heads", "rows"), None)
    qkv = P(None, "rows", "heads")
    tall = P("heads", "rows")
    wide = P("rows", "heads")
    placed = (
        group,
        P("rows"),
        group,
        group,
        P(),
        P("rows"),
        P(None, "heads", None, None),
        *(table,) * 4,
        *(qkv,) * 4,
        *(tall,) * 4,
        *(wide,) * 4,
        *(tall,) * 4,
        *(P(),) * 8,
    )
    return jax.shard_map(
        per_device,
        mesh=mesh,
        in_specs=placed,
        out_specs=(
            P(),
            *(table,) * 3,
            *(qkv,) * 3,
            *(tall,) * 3,
            *(wide,) * 3,
            *(tall,) * 3,
            *(P(),) * 6,
        ),
        check_vma=False,
    )
```

```python
import jax
import jax.numpy as jnp
from jax import lax
from jax.experimental import pallas as pl
from jax.sharding import PartitionSpec as P

D = 768
HDIM = 64
SEQ = 256
NLW = 4
CGIT = 8
STATS = 16

EPS_NORM = 1e-05
BETA_ONE = 0.9
BETA_TWO = 0.999
ADAM_EPS = 1e-08
LEARN_RATE = 0.03
DECAY_RATE = 0.01
CLIP_NORM = 1.0
CG_SHIFT = 0.002
MASKED = -1e30
HALF_ROOT = 0.7071067811865476
INV_ROOT_TAU = 0.3989422804014327
HIGH = lax.Precision.HIGHEST
ALL = ("heads", "rows")
LOW = jnp.bfloat16


def einsum(form, left, right):
    return jnp.einsum(form, left, right, preferred_element_type=jnp.float32)


def gelu_slope(values):
    return (
        0.5 * (1.0 + lax.erf(values * HALF_ROOT))
        + values * jnp.exp(-0.5 * values * values) * INV_ROOT_TAU
    )


def norm_pair(values, dots, gain, bias, gain_dot, bias_dot):
    center = values - jnp.mean(values, axis=-1, keepdims=True)
    inverse = lax.rsqrt(jnp.mean(center * center, axis=-1, keepdims=True) + EPS_NORM)
    normed = center * inverse
    normed_dot = inverse * (
        dots
        - jnp.mean(dots, axis=-1, keepdims=True)
        - normed * jnp.mean(normed * dots, axis=-1, keepdims=True)
    )
    return (normed * gain + bias, normed_dot * gain + normed * gain_dot + bias_dot, normed, inverse)


def norm_backward(grad_out, normed, inverse, gain):
    scaled = grad_out * gain
    grad_in = inverse * (
        scaled
        - jnp.mean(scaled, axis=-1, keepdims=True)
        - normed * jnp.mean(scaled * normed, axis=-1, keepdims=True)
    )
    return (grad_in, jnp.sum(grad_out * normed, axis=0), jnp.sum(grad_out, axis=0))


def everyone(block):
    count = lax.axis_size(ALL[0]) * lax.axis_size(ALL[1])
    return lax.all_to_all(
        jnp.broadcast_to(block, (count, block.shape[1])), ALL, 0, 0, tiled=True
    )


def bits_of(axis):
    return [(axis, bit) for bit in reversed(range(lax.axis_size(axis).bit_length() - 1))]


def owned(parts):
    layout = [bit for axis in ALL for bit in bits_of(axis)]
    first = (ALL[0], 0)
    last = [bit for bit in layout if bit[0] == ALL[1] and bit[1] >= 2]
    middle = [bit for bit in layout if bit != first and bit not in last]
    results = []
    for turn, part in enumerate(parts):
        turn %= len(middle)
        order = [first] + middle[turn:] + middle[:turn] + last[::-1]
        left = list(layout)
        block = part.reshape((2,) * len(layout) + (-1, part.shape[-1]))
        for step in order:
            axis, bit = step
            place = left.index(step)
            mine = (lax.axis_index(axis) >> bit) & 1
            send = lax.dynamic_index_in_dim(block, 1 - mine, place, keepdims=False)
            keep = lax.dynamic_index_in_dim(block, mine, place, keepdims=False)
            size = lax.axis_size(axis)
            came = lax.ppermute(send, axis, [(index, index ^ (1 << bit)) for index in range(size)])
            block = keep.astype(jnp.float32) + came.astype(jnp.float32)
            left.pop(place)
            if left:
                block = block.astype(LOW)
        results.append(block)
    return results


def solve_kernel(stats_ref, feat_ref, targets_ref, coef_ref, norm_ref, loss_ref):
    count = feat_ref.shape[0]

    def stat(index):
        return stats_ref[:, index * count : (index + 1) * count]

    peaks = stat(0)
    peak = jnp.max(peaks, axis=0, keepdims=True)
    scale = jnp.exp(peaks - peak)
    mass = jnp.sum(stat(1) * scale, axis=0, keepdims=True)
    weighted = jnp.sum(stat(2) * scale, axis=0, keepdims=True)
    log_norm = peak + jnp.log(mass)
    shift = log_norm + weighted / mass
    picked = [
        jnp.sum(stat(3 + word) + stat(3 + NLW + word), axis=0, keepdims=True)
        for word in range(NLW)
    ]
    differ = jnp.concatenate(picked, axis=0) - shift - targets_ref[...]
    feat = feat_ref[...].astype(jnp.float32)
    center = feat - jnp.mean(feat, axis=0, keepdims=True)
    kernel = (
        lax.dot_general(
            center,
            center,
            (((1,), (1,)), ((), ())),
            precision=HIGH,
            preferred_element_type=jnp.float32,
        )
        / D
    )
    answer = jnp.zeros_like(differ)
    residual = differ
    direction = differ
    norm_now = jnp.sum(residual * residual, axis=1, keepdims=True)
    for step in range(CGIT):
        image = (
            jnp.dot(direction, kernel, precision=HIGH, preferred_element_type=jnp.float32)
            + CG_SHIFT * direction
        )
        alpha = norm_now / jnp.sum(direction * image, axis=1, keepdims=True)
        answer = answer + alpha * direction
        residual = residual - alpha * image
        if step + 1 < CGIT:
            norm_next = jnp.sum(residual * residual, axis=1, keepdims=True)
            direction = residual + norm_next / norm_now * direction
            norm_now = norm_next
    coef_ref[...] = 2.0 * answer / NLW
    norm_ref[...] = log_norm
    squares = jnp.sum(differ * differ, axis=1, keepdims=True)
    loss_ref[...] = jnp.sum(squares, axis=0, keepdims=True) / NLW


def solve(stats, feat, targets):
    count = feat.shape[0]
    return pl.pallas_call(
        solve_kernel,
        out_shape=(
            jax.ShapeDtypeStruct((NLW, count), jnp.float32),
            jax.ShapeDtypeStruct((1, count), jnp.float32),
            jax.ShapeDtypeStruct((1, 1), jnp.float32),
        ),
    )(stats, feat, targets)


def adam_moments(gradient, moment_one, moment_two, bias_one, bias_two):
    new_one = BETA_ONE * moment_one + (1.0 - BETA_ONE) * gradient
    new_two = BETA_TWO * moment_two + (1.0 - BETA_TWO) * gradient * gradient
    return (new_one / bias_one / (jnp.sqrt(new_two / bias_two) + ADAM_EPS), new_one, new_two)


def adam_update(master, gradient, moment_one, moment_two, clip_scale, bias_one, bias_two):
    direction, new_one, new_two = adam_moments(
        clip_scale * gradient, moment_one, moment_two, bias_one, bias_two
    )
    return (master - LEARN_RATE * (direction + DECAY_RATE * master), new_one, new_two)


def turned_update(owner, master, gradient, first, second, basis, clip_scale, bias_one, bias_two):
    count, height, width = gradient.shape

    def grouped(array):
        return array.reshape(count, height, width // HDIM, HDIM)

    plain = clip_scale * gradient
    turned = jnp.einsum("ciha,chab->cihb", grouped(plain), basis, precision=HIGH)
    used = jnp.where(owner, turned.reshape(gradient.shape), plain)
    direction, new_one, new_two = adam_moments(used, first, second, bias_one, bias_two)
    back = jnp.einsum("cihb,chab->ciha", grouped(direction), basis, precision=HIGH)
    direction = jnp.where(owner, back.reshape(gradient.shape), direction)
    return (master - LEARN_RATE * (direction + DECAY_RATE * master), new_one, new_two)


def per_device(
    token_ids,
    lengths,
    label_ids,
    targets,
    step_count,
    soap_owners,
    soap_basis,
    table_anchor,
    table_delta,
    table_first,
    table_second,
    qkv_anchor,
    qkv_delta,
    qkv_first,
    qkv_second,
    out_anchor,
    out_delta,
    out_first,
    out_second,
    up_anchor,
    up_delta,
    up_first,
    up_second,
    down_anchor,
    down_delta,
    down_first,
    down_second,
    gain_anchor,
    gain_delta,
    gain_first,
    gain_second,
    bias_anchor,
    bias_delta,
    bias_first,
    bias_second,
):
    n_heads = lax.axis_size("heads")
    n_rows = lax.axis_size("rows")
    count = n_heads * n_rows
    head_index = lax.axis_index("heads")
    me = head_index * n_rows + lax.axis_index("rows")
    vocab = table_anchor.shape[0]
    group_wide = qkv_anchor.shape[2]
    local_heads = group_wide // HDIM

    def side_by_side(qkv, out):
        return jnp.concatenate([qkv[0], qkv[1], qkv[2], out.T], axis=1)

    def gathered(anchor, delta):
        block = jnp.concatenate([anchor, delta.astype(LOW)], axis=1)
        full = lax.all_gather(block, ALL, axis=0, tiled=True)
        return full.reshape(n_heads, D, block.shape[1])

    attn_all = gathered(side_by_side(qkv_anchor, out_anchor), side_by_side(qkv_delta, out_delta))
    ffn_all = gathered(
        jnp.concatenate([up_anchor, down_anchor.T], axis=1),
        jnp.concatenate([up_delta, down_delta.T], axis=1),
    )

    room = 8 * -(-(2 * SEQ // count + 8) // 8)
    slots = count * room
    ids = lax.dynamic_index_in_dim(token_ids, head_index, 0, keepdims=False)
    owner = ids // vocab
    local = ids - owner * vocab
    place = lax.iota(jnp.int32, SEQ)
    same = ids[:, None] == ids[None, :]
    earliest = jnp.min(jnp.where(same, place[None, :], SEQ), axis=1)
    leads = earliest == place
    rank = jnp.sum(
        (leads[None, :] & (owner[:, None] == owner[None, :]) & (place[None, :] < earliest[:, None])),
        axis=1,
        dtype=jnp.int32,
    )
    longest = jnp.max(rank) + 1
    own_labels = lax.dynamic_index_in_dim(label_ids, head_index, 0, keepdims=False)
    own_targets = lax.dynamic_index_in_dim(targets, head_index, 0, keepdims=False)
    notes = jnp.concatenate(
        [longest[None].astype(jnp.float32), own_labels.astype(jnp.float32), own_targets]
    )
    both = jnp.concatenate([table_anchor, table_delta.astype(LOW)], axis=1)

    def slot_of(turn):
        within = rank - turn * room
        return jnp.where((within >= 0) & (within < room), owner * room + within, -1)

    def wanted_of(turn):
        taken = jnp.where(leads, slot_of(turn), -1)
        hit = lax.iota(jnp.int32, slots)[:, None] == taken[None, :]
        return (jnp.sum(jnp.where(hit, local[None, :] + 1, 0), axis=1) - 1).reshape(count, room)

    def asked(turn):
        return lax.all_to_all(wanted_of(turn), ALL, 0, 0, tiled=True).reshape(slots)

    def chosen(wanted):
        return (wanted[:, None] == lax.broadcasted_iota(jnp.int32, (slots, vocab), 1)).astype(LOW)

    def token_slots(turn):
        return (
            slot_of(turn)[:, None] == lax.broadcasted_iota(jnp.int32, (SEQ, slots), 1)
        ).astype(LOW)

    def fetch(turn, wanted):
        rows = einsum("sv,vd->sd", chosen(wanted), both).astype(LOW)
        rows = lax.all_to_all(rows.reshape(count, room, 2 * D), ALL, 0, 0, tiled=True)
        return einsum("ts,sd->td", token_slots(turn), rows.reshape(slots, 2 * D))

    def give(turn, wanted, grads):
        sums = einsum("ts,td->sd", token_slots(turn), grads).astype(LOW)
        sums = lax.all_to_all(sums.reshape(count, room, D), ALL, 0, 0, tiled=True)
        return einsum("sv,sd->vd", chosen(wanted), sums.reshape(slots, D))

    def more(start, step):
        def rest(value):
            return lax.fori_loop(1, rounds, lambda turn, so_far: so_far + step(turn), value)

        return lax.cond(rounds > 1, rest, lambda value: value, start)

    message = jnp.concatenate(
        [
            wanted_of(0).astype(jnp.float32),
            jnp.broadcast_to(notes[None], (count, notes.shape[0])),
        ],
        axis=1,
    )
    message = lax.all_to_all(message, ALL, 0, 0, tiled=True)
    wanted_first = message[:, :room].astype(jnp.int32).reshape(slots)
    rounds = -(-jnp.max(message[:, room]).astype(jnp.int32) // room)
    labels = message[:, room + 1 : room + 1 + NLW].astype(jnp.int32) - me * vocab
    targets_all = message[:, room + 1 + NLW :].T
    embedded_both = more(fetch(0, wanted_first), lambda turn: fetch(turn, asked(turn)))
    start_x, start_dot, normed_zero, inverse_zero = norm_pair(
        embedded_both[:, :D],
        embedded_both[:, D:],
        gain_anchor[0],
        bias_anchor[0],
        gain_delta[0],
        bias_delta[0],
    )

    own_length = lax.dynamic_index_in_dim(lengths, head_index, 0, keepdims=False)
    live = lax.iota(jnp.int32, SEQ) < own_length
    length_float = own_length.astype(jnp.float32)

    attn_in = start_x.astype(LOW)
    attn_dot_in = start_dot.astype(LOW)
    three = 3 * group_wide
    wide = attn_all.shape[2] // 2
    through = einsum("td,hde->the", attn_in, attn_all)
    projected = through[:, :, :three].astype(LOW)
    projected_dot = (
        through[:, :, wide : wide + three]
        + einsum("td,hde->the", attn_dot_in, attn_all[:, :, :three])
    ).astype(LOW)

    def split_heads(array):
        array = array.reshape(SEQ, n_heads, 3, local_heads, HDIM)
        return [array[:, :, index].reshape(SEQ, n_heads * local_heads, HDIM) for index in range(3)]

    query, key, value = split_heads(projected)
    query_dot, key_dot, value_dot = split_heads(projected_dot)
    scores = einsum("qhd,khd->hqk", query, key) * HDIM ** (-0.5)
    scores = jnp.where(live[None, None, :], scores, MASKED)
    exponent = jnp.exp(scores - jnp.max(scores, axis=-1, keepdims=True))
    probs = exponent / jnp.sum(exponent, axis=-1, keepdims=True)
    probs_low = probs.astype(LOW)
    score_dot = (
        einsum("qhd,khd->hqk", query_dot, key) + einsum("qhd,khd->hqk", query, key_dot)
    ) * HDIM ** (-0.5)
    prob_dot = (probs * (score_dot - jnp.sum(probs * score_dot, axis=-1, keepdims=True))).astype(LOW)
    attended = einsum("hqk,khd->qhd", probs_low, value).astype(LOW)
    attended_dot = (
        einsum("hqk,khd->qhd", prob_dot, value) + einsum("hqk,khd->qhd", probs_low, value_dot)
    ).astype(LOW)
    attended = attended.reshape(SEQ, n_heads, group_wide)
    attended_dot = attended_dot.reshape(SEQ, n_heads, group_wide)
    out_full = attn_all[:, :, three:wide]
    out_step = attn_all[:, :, wide + three :]
    attn_out = einsum("the,hde->td", attended, out_full)
    attn_dot = einsum("the,hde->td", attended_dot, out_full) + einsum(
        "the,hde->td", attended, out_step
    )
    hidden, hidden_dot, normed_one, inverse_one = norm_pair(
        start_x + attn_out,
        start_dot + attn_dot,
        gain_anchor[1],
        bias_anchor[1],
        gain_delta[1],
        bias_delta[1],
    )
    ffn_input = hidden.astype(LOW)
    up_full, down_full, up_step, down_step = jnp.split(ffn_all, 4, axis=2)
    pre_gelu = einsum("td,hde->the", ffn_input, up_full)
    pre_dot = einsum("td,hde->the", hidden_dot.astype(LOW), up_full) + einsum(
        "td,hde->the", ffn_input, up_step
    )
    activated = jax.nn.gelu(pre_gelu, approximate=False).astype(LOW)
    slope = gelu_slope(pre_gelu)
    act_dot = (slope * pre_dot).astype(LOW)
    ffn_out = einsum("the,hde->td", activated, down_full)
    ffn_dot = einsum("the,hde->td", act_dot, down_full) + einsum(
        "the,hde->td", activated, down_step
    )
    final_out, final_dot, normed_two, inverse_two = norm_pair(
        hidden + ffn_out,
        hidden_dot + ffn_dot,
        gain_anchor[2],
        bias_anchor[2],
        gain_delta[2],
        bias_delta[2],
    )

    def pooled(values):
        return (jnp.sum(jnp.where(live[:, None], values, 0.0), axis=0) / length_float).astype(LOW)

    feats = everyone(jnp.concatenate([pooled(final_dot), pooled(final_out)])[None])
    feat_all = feats[:, D:]
    logits = einsum("gd,vd->gv", feat_all, table_anchor)
    logit_dot = einsum("gd,vd->gv", feats, both)
    vocab_iota = lax.broadcasted_iota(jnp.int32, logits.shape, 1)
    marks = [vocab_iota == labels[:, word : word + 1] for word in range(NLW)]
    peak_local = jnp.max(logits, axis=1)
    exponent = jnp.exp(logits - peak_local[:, None])
    stats = [peak_local, jnp.sum(exponent, axis=1), jnp.sum(exponent * logit_dot, axis=1)]
    stats += [jnp.sum(jnp.where(mark, logits, 0.0), axis=1) for mark in marks]
    stats += [jnp.sum(jnp.where(mark, logit_dot, 0.0), axis=1) for mark in marks]
    stats += [jnp.zeros_like(peak_local)] * (STATS - len(stats))
    stats = everyone(jnp.stack(stats).reshape(1, STATS * count))
    coefficient, log_norm, loss_value = solve(stats, feat_all, targets_all)
    coefficient = coefficient.T
    grad_logits = -jnp.sum(coefficient, axis=1, keepdims=True) * jnp.exp(logits - log_norm.T)
    for word, mark in enumerate(marks):
        grad_logits = grad_logits + jnp.where(mark, coefficient[:, word : word + 1], 0.0)
    grad_logits = grad_logits.astype(LOW)
    grad_feat = einsum("gv,vd->gd", grad_logits, table_anchor)
    grad_feat = jnp.sum(lax.all_to_all(grad_feat, ALL, 0, 0, tiled=True), axis=0)

    grad_final = jnp.where(live[:, None], (grad_feat / length_float)[None, :], 0.0)
    grad_two, gain_two, bias_two_grad = norm_backward(
        grad_final, normed_two, inverse_two, gain_anchor[2]
    )

    grad_ffn = grad_two.astype(LOW)
    grad_down = einsum("td,the->hde", grad_ffn, activated).astype(LOW)
    grad_act = einsum("td,hde->the", grad_ffn, down_full)
    grad_pre = (slope * grad_act).astype(LOW)
    grad_up = einsum("td,the->hde", ffn_input, grad_pre).astype(LOW)
    grad_hidden = grad_two + einsum("the,hde->td", grad_pre, up_full)
    grad_one, gain_one, bias_one_grad = norm_backward(
        grad_hidden, normed_one, inverse_one, gain_anchor[1]
    )
    grad_attn = grad_one.astype(LOW)
    grad_out = einsum("td,the->hde", grad_attn, attended).astype(LOW)
    grad_att = einsum("td,hde->the", grad_attn, out_full).astype(LOW)
    grad_att = grad_att.reshape(SEQ, n_heads * local_heads, HDIM)
    grad_prob = einsum("qhd,khd->hqk", grad_att, value)
    grad_value = einsum("hqk,qhd->khd", probs_low, grad_att)
    delta_sum = jnp.sum(probs * grad_prob, axis=-1, keepdims=True)
    grad_score = (probs * (grad_prob - delta_sum)).astype(LOW)
    grad_query = einsum("hqk,khd->qhd", grad_score, key) * HDIM ** (-0.5)
    grad_key = einsum("hqk,qhd->khd", grad_score, query) * HDIM ** (-0.5)
    grad_rows = jnp.concatenate(
        [
            part.astype(LOW).reshape(SEQ, n_heads, group_wide)
            for part in (grad_query, grad_key, grad_value)
        ],
        axis=2,
    )
    grad_qkv = einsum("td,the->hde", attn_in, grad_rows).astype(LOW)
    grad_attn_all = jnp.concatenate([grad_qkv, grad_out], axis=2)
    grad_down, grad_up, grad_attn_all = owned([grad_down, grad_up, grad_attn_all])
    grad_start = grad_one + einsum("the,hde->td", grad_rows, attn_all[:, :, :three])
    grad_embed, gain_zero, bias_zero = norm_backward(
        grad_start, normed_zero, inverse_zero, gain_anchor[0]
    )
    grad_embed = grad_embed.astype(LOW)
    table_term = einsum("gv,gd->vd", grad_logits, feat_all) + give(0, wanted_first, grad_embed)
    table_grad = more(table_term, lambda turn: give(turn, asked(turn), grad_embed))

    norm_grads = jnp.stack(
        [gain_zero, gain_one, gain_two, bias_zero, bias_one_grad, bias_two_grad]
    )
    pieces = lax.all_to_all(norm_grads.reshape(count, -1), ALL, 0, 0, tiled=True)
    piece = jnp.sum(pieces, axis=0, keepdims=True)
    squares = sum(
        jnp.sum(part * part) for part in (table_grad, grad_attn_all, grad_up, grad_down, piece)
    )
    shared = everyone(jnp.concatenate([jnp.broadcast_to(squares, (1, 128)), piece], axis=1))
    gain_grad, bias_grad = shared[:, 128:].reshape(2, 3, D)
    squares = jnp.sum(shared[:, 0])
    clip_scale = jnp.minimum(1.0, CLIP_NORM / jnp.sqrt(squares))
    steps_done = step_count[0].astype(jnp.float32)
    bias_one = 1.0 - jnp.power(BETA_ONE, steps_done)
    bias_two = 1.0 - jnp.power(BETA_TWO, steps_done)
    rates = (clip_scale, bias_one, bias_two)

    def with_out(qkv, out):
        return jnp.concatenate([qkv, out.T[None]], axis=0)

    height = qkv_delta.shape[1]
    turned = turned_update(
        soap_owners[0] == 1,
        with_out(qkv_delta, out_delta),
        jnp.swapaxes(grad_attn_all.reshape(height, 4, group_wide), 0, 1),
        with_out(qkv_first, out_first),
        with_out(qkv_second, out_second),
        soap_basis,
        *rates,
    )
    return (
        loss_value[0, 0],
        *adam_update(table_delta, table_grad, table_first, table_second, *rates),
        *(part[:3] for part in turned),
        *(part[3].T for part in turned),
        *adam_update(up_delta, grad_up, up_first, up_second, *rates),
        *adam_update(down_delta, grad_down.T, down_first, down_second, *rates),
        *adam_update(gain_delta, gain_grad, gain_first, gain_second, *rates),
        *adam_update(bias_delta, bias_grad, bias_first, bias_second, *rates),
    )


def solution(mesh):
    group = P("rows", None)
    table = P(("heads", "rows"), None)
    qkv = P(None, "rows", "heads")
    tall = P("heads", "rows")
    wide = P("rows", "heads")
    placed = (
        group,
        P("rows"),
        group,
        group,
        P(),
        P("rows"),
        P(None, "heads", None, None),
        *(table,) * 4,
        *(qkv,) * 4,
        *(tall,) * 4,
        *(wide,) * 4,
        *(tall,) * 4,
        *(P(),) * 8,
    )
    return jax.shard_map(
        per_device,
        mesh=mesh,
        in_specs=placed,
        out_specs=(
            P(),
            *(table,) * 3,
            *(qkv,) * 3,
            *(tall,) * 3,
            *(wide,) * 3,
            *(tall,) * 3,
            *(P(),) * 6,
        ),
        check_vma=False,
    )
```
